256 devices in a mesh: lon: 64 (over y_lo, z, x), lat: 4 (over y_hi, core).
Axes of the slice: x: 4, y: 4 (y_hi: 2, y_lo: 2; y = y_hi * 2 + y_lo), z: 8, core: 2. Of those that a mesh axis runs over, the one named last changes fastest.
Arguments:
- observed: float32 [2, 4096, 1024], P(None, 'lon', 'lat')
- kappa_squared: float32 [2, 4096, 1024], P(None, 'lon', 'lat'), may hold values from 0.05 to 4
- probe_bits: int32 [2, 2, 4096, 1024], P(None, None, 'lon', 'lat'), may hold values from 0 to 255
- land_sea: int32 [4096, 1024], P('lon', 'lat'), may hold values from 0 to 1, as said below
- coarse_block_inverse: float32 [2, 32, 2, 32], replicated, as said below
Outputs:
- solution: float32 [2, 4096, 1024], P(None, 'lon', 'lat')
- diagonal_estimate: float32 [2, 4096, 1024], P(None, 'lon', 'lat')
- holdout_residual: float32 [2, 4096, 1024], P(None, 'lon', 'lat')
The draws below stay inside these ranges and needn't reach their ends.
Inputs may be any that keep to these rules, and one draw needn't show every extreme that they name: `land_sea`: 1 marks an ocean cell, 0 land. `coarse_block_inverse`: symmetric and positive definite as a matrix of 64 rows.
All inputs are finite; a program needn't handle non-finite values.
Results may differ from the reference program's by a relative error of at most 0.0003.
Values sent between devices are 32-bit elements; how exact they have to be, the bound alone decides.
No kernel may reach another device: no remote copies, remote signals or barrier semaphores. Data moves between devices by JAX's collectives and lax.ppermute only.
A program may use at most 128 MiB of HBM per device.

```python
import math
import jax
import jax.numpy as jnp
from jax import lax

LEV = 2
BLK = 32
PROBES = 16
ITERS = 2
NLON = 4096
NLAT = 1024
NCLAT = 32
WORDS = 2


def draw_observed(key, part):
    noise = jax.random.normal(key, (LEV, NLON, NLAT), jnp.float32)
    return jnp.clip(noise, -6.0, 6.0)


def draw_land_sea(key, part):
    shape = (NLON, NLAT)
    ticket = jax.random.randint(key, shape, 0, 1000, dtype=jnp.int32)
    lon_pos = lax.broadcasted_iota(jnp.int32, shape, 0)
    lat_pos = lax.broadcasted_iota(jnp.int32, shape, 1)
    limit = 250 + 350 * lon_pos // NLON + 300 * lat_pos // NLAT
    return (ticket < limit).astype(jnp.int32)


def draw_coarse_block_inverse(key, part):
    order = LEV * NCLAT
    spread = jax.random.uniform(key, (order, order), jnp.float32, -1.0, 1.0)
    off_diagonal = 0.25 * (spread + spread.T) / order
    diag_vals = jax.random.uniform(jax.random.fold_in(key, 7), (order,), jnp.float32, 0.5, 1.0)
    rows = lax.broadcasted_iota(jnp.int32, (order, order), 0)
    cols = lax.broadcasted_iota(jnp.int32, (order, order), 1)
    unit = (rows == cols).astype(jnp.float32)
    whole_field = (off_diagonal * (1.0 - unit) + unit * diag_vals[:, None]) / (BLK * BLK)
    return whole_field.reshape(LEV, NCLAT, LEV, NCLAT)


def plant(result, rng, low, largest):
    longest = result.shape.index(max(result.shape))
    spots = []
    for shift in (0, 1):
        where = [jax.random.randint(jax.random.fold_in(rng, axis), (), 0, length) for axis, length in enumerate(result.shape)]
        where[longest] = (where[longest] + shift) % result.shape[longest]
        spots.append(tuple(where))
    return result.at[spots[0]].set(low).at[spots[1]].set(largest)


def shard_levels(key, extent, pieces, low, top_value):
    def one(axis_at, shards_of):
        draws = jax.random.uniform(jax.random.fold_in(jax.random.fold_in(key, 6), axis_at), (shards_of,), jnp.float32, low / len(pieces), top_value / len(pieces))
        return jnp.repeat(jnp.exp(draws), extent[axis_at] // shards_of).reshape((-1,) + (1,) * (len(extent) - axis_at - 1))

    level = one(*pieces[0])
    for cut in pieces[1:]:
        level = level * one(*cut)
    return level


def setup_inputs(seed: int = 0) -> dict:
    keys = jax.random.split(jax.random.key(seed), 6)
    return {
        "observed": draw_observed(jax.random.fold_in(keys[5], 71), 0),
        "kappa_squared": jnp.clip(jnp.exp(math.log(4.0) - 4.3820266 * jax.random.uniform(keys[1], (LEV, NLON, NLAT), jnp.float32) ** shard_levels(keys[1], (LEV, NLON, NLAT), ((1, 64), (2, 4)), -0.2, 0.2)), 0.05, 4.0),
        "probe_bits": plant(jax.random.randint(keys[2], (WORDS, LEV, NLON, NLAT), 0, 256), jax.random.fold_in(keys[2], 1), 0, 255).astype(jnp.int32),
        "land_sea": draw_land_sea(jax.random.fold_in(keys[5], 71), 0),
        "coarse_block_inverse": draw_coarse_block_inverse(jax.random.fold_in(keys[5], 71), 0),
    }


def reference(observed, kappa_squared, probe_bits, land_sea, coarse_block_inverse):
    ocean = land_sea.astype(jnp.float32)
    coef = kappa_squared + 5.0
    jacobi = ocean / (coef * coef + 4.0)

    def apply_k(field):
        beside = jnp.roll(field, 1, axis=1) + jnp.roll(field, -1, axis=1)
        padded = jnp.pad(field, ((0, 0), (0, 0), (1, 1)))
        beside = beside + padded[:, :, :-2] + padded[:, :, 2:]
        levels = jnp.pad(field, ((1, 1), (0, 0), (0, 0)))
        vertical = levels[:-2] + levels[2:]
        return ocean * (coef * field - beside - 0.5 * vertical)

    def precondition(resid):
        blocks = resid.reshape(LEV, NLON // BLK, BLK, NCLAT, BLK).sum(axis=(2, 4))
        correction = jnp.einsum("mclb,lab->mac", coarse_block_inverse, blocks, precision=lax.Precision.HIGHEST)
        spread = jnp.broadcast_to(correction[:, :, None, :, None], (LEV, NLON // BLK, BLK, NCLAT, BLK))
        return jacobi * resid + ocean * spread.reshape(LEV, NLON, NLAT)

    def right_side(index):
        shifted = jnp.maximum(index - 1, 0)
        word = probe_bits[shifted // 8]
        bit_value = jnp.right_shift(word, shifted % 8) & 1
        signs = (2 * bit_value - 1).astype(jnp.float32)
        return ocean * jnp.where(index == 0, observed, signs)

    def solve(rhs):
        resid = rhs
        precond = precondition(resid)
        gamma = jnp.sum(resid * precond)
        direction = precond
        answer = jnp.zeros_like(rhs)
        for step in range(ITERS):
            image = apply_k(apply_k(direction))
            alpha = gamma / jnp.sum(direction * image)
            answer = answer + alpha * direction
            if step + 1 < ITERS:
                resid = resid - alpha * image
                precond = precondition(resid)
                gamma_new = jnp.sum(resid * precond)
                direction = precond + (gamma_new / gamma) * direction
                gamma = gamma_new
        return answer

    def system_step(carry, index):
        first, total = carry
        rhs = right_side(index)
        answer = solve(rhs)
        first = jnp.where(index == 0, answer, first)
        weight = jnp.where(index == 0, jnp.float32(0.0), jnp.float32(1.0))
        total = total + weight * (rhs * answer)
        return (first, total), None

    zeros = jnp.zeros((LEV, NLON, NLAT), jnp.float32)
    (solution, total), _ = lax.scan(system_step, (zeros, zeros), jnp.arange(PROBES + 1, dtype=jnp.int32))
    diagonal_estimate = total / PROBES
    lower_bound_value = 0.5 / (coef * coef + 4.0)
    holdout_residual = solution / jnp.maximum(diagonal_estimate, lower_bound_value)
    return solution, diagonal_estimate, holdout_residual
```

```python
import functools

import jax
import jax.numpy as jnp
from jax import lax
from jax.experimental import pallas as pl
from jax.experimental.pallas import tpu as pltpu
from jax.sharding import PartitionSpec as P

BLK = 32
PROBES = 16
HALO = 3
TOP = 8
LANES = 128
EXACT = lax.Precision.HIGHEST
F32 = jnp.float32


def vmem(count):
    return [pl.BlockSpec(memory_space=pltpu.VMEM)] * count


def shape(*dims):
    return jax.ShapeDtypeStruct(dims, F32)


def iota(dims, axis):
    return lax.broadcasted_iota(jnp.int32, dims, axis)


def same_row(ref, row, stride):
    found = []
    for tile in range(ref.shape[0]):
        if stride == 0:
            found.append(jnp.broadcast_to(ref[tile, pl.ds(row, 1), :], (8, LANES)))
        else:
            found.append(ref[tile, pl.ds(row, 8, stride=stride), :])
    return jnp.concatenate(found, axis=1)


def keep(ref, value):
    for tile in range(ref.shape[0]):
        ref[tile] = value[:, tile * LANES : tile * LANES + LANES]


def row_of(ref, row):
    return jnp.broadcast_to(ref[pl.ds(row, 1), :], (8, ref.shape[1]))


def block_lanes(lat_at, level, width):
    source = iota((width, LANES), 0)
    lane = iota((width, LANES), 1)
    return jnp.where(lane == 64 + 16 * lat_at + 8 * level + source // BLK, 1.0, 0.0).astype(F32)


def block_sums(lat_at, rows):
    total = None
    for level in range(2):
        part = jnp.dot(
            rows[level],
            block_lanes(lat_at, level, rows[level].shape[1]),
            precision=EXACT,
            preferred_element_type=F32,
        )
        total = part if total is None else total + part
    return total


def first_row(row):
    return jnp.where(iota((8, row.shape[1]), 0) == 0, jnp.broadcast_to(row, (8, row.shape[1])), 0.0)


def raw_fields(obs, kap, bits, land):
    return (
        [obs[level] for level in range(2)]
        + [kap[level] for level in range(2)]
        + [bits[word, level].astype(F32) for word in range(2) for level in range(2)]
        + [land[...].astype(F32)]
    )


def prepare_kernel(obs, kap, bits, land, to_prev, to_next, own, ocean):
    lat_at = lax.axis_index("lat")
    lon_rows, width = land.shape
    fields = raw_fields(obs, kap, bits, land)
    lane = iota((lon_rows, LANES), 1)
    edges = jnp.zeros((lon_rows, LANES), F32)
    to_prev[...] = jnp.zeros(to_prev.shape, F32)
    to_next[...] = jnp.zeros(to_next.shape, F32)
    for at, field in enumerate(fields):
        to_prev[HALO * at : HALO * at + HALO, :] = field[:HALO]
        to_next[HALO * at : HALO * at + HALO, :] = field[lon_rows - HALO :]
        low = pltpu.roll(field[:, :LANES], 6 * at, 1) if at else field[:, :LANES]
        high = pltpu.roll(field[:, width - LANES :], (6 * at + 6) % LANES, 1)
        edges = jnp.where((lane >= 6 * at) & (lane < 6 * at + 3), low, edges)
        edges = jnp.where((lane >= 6 * at + 3) & (lane < 6 * at + 6), high, edges)
    to_prev[27:30, :LANES] = edges[:HALO]
    to_next[27:30, :LANES] = edges[lon_rows - HALO :]
    keep(ocean, fields[8])
    bit = jnp.left_shift(1, iota((8, width), 0))
    sums = {}
    for column in range(2):

        def body(row, carry):
            wet = same_row(ocean, row, 0)
            out = []
            for word in range(2):
                for level in range(2):
                    held = row_of(bits.at[word, level], row)
                    out.append(carry[word * 2 + level] + jnp.where((held & bit) != 0, wet, -wet))
            return tuple(out)

        zero = jnp.zeros((8, width), F32)
        got = lax.fori_loop(column * BLK, column * BLK + BLK, body, (zero,) * 4, unroll=4)
        for word in range(2):
            for level in range(2):
                sums[column, word, level] = got[word * 2 + level]
        for level in range(2):
            held = slice(column * BLK, column * BLK + BLK)
            sums[column, 2, level] = first_row(
                jnp.sum(fields[8][held] * fields[level][held], axis=0, keepdims=True)
            )
    rows = [
        jnp.concatenate([sums[column, group, level] for column in range(2) for group in range(3)], axis=0)
        for level in range(2)
    ]
    found = block_sums(lat_at, rows)
    own[...] = jnp.zeros(own.shape, F32)
    own[TOP : TOP + lon_rows, :] = edges
    own[24:72, :] = own[24:72, :] + found
    for target, at in ((to_prev, 0), (to_next, 24)):
        target[32:40, :LANES] = found[at : at + 8]
        target[32:40, LANES : 2 * LANES] = found[at + 8 : at + 16]
        target[40:48, :LANES] = found[at + 16 : at + 24]


def merge_kernel(own, from_prev, from_next, out):
    out[...] = own[...]
    for source, row, at in ((from_prev, TOP - HALO, 0), (from_next, TOP + 64, 72)):
        out[row : row + HALO, :] = out[row : row + HALO, :] + source[27:30, :LANES]
        out[at : at + 8, :] = out[at : at + 8, :] + source[32:40, :LANES]
        out[at + 8 : at + 16, :] = out[at + 8 : at + 16, :] + source[32:40, LANES : 2 * LANES]
        out[at + 16 : at + 24, :] = out[at + 16 : at + 24, :] + source[40:48, :LANES]


def spread_kernel(coarse, spread):
    lat_at = lax.axis_index("lat")
    wide = spread.shape[2]
    own = wide - LANES
    per = own // BLK
    lane = iota((32, wide), 1)
    block = jnp.where(lane < own, lane // BLK, -1000)
    block = jnp.where((lane >= own) & (lane < own + HALO), per, block)
    block = jnp.where(lane >= wide - HALO, -1, block)
    chosen = jnp.where(iota((32, wide), 0) == block + per * lat_at, 1.0, 0.0).astype(F32)
    for level in range(2):
        spread[level, 0:64, :] = jnp.zeros((64, wide), F32)
        for other in range(2):
            part = lax.dot_general(
                coarse[level, :, other, :],
                chosen,
                (((0,), (0,)), ((), ())),
                precision=EXACT,
                preferred_element_type=F32,
            )
            for group in range(4):
                at = 64 + 16 * group + 8 * other
                spread[level, at : at + 8, :] = part[8 * group : 8 * group + 8]


def corrections(gathered, spread, probe_part, first_part):
    total = gathered[0] + gathered[1] + gathered[2] + gathered[3]
    total = jnp.where(iota(total.shape, 1) >= 64, total, 0.0)
    for level in range(2):
        found = jnp.dot(total, spread[level], precision=EXACT, preferred_element_type=F32)
        probe_part[level] = found
        wide = found.shape[1]
        for low, high, at in ((TOP - HALO, TOP, 16), (TOP, 40, 40), (40, 72, 64), (72, 72 + HALO, 88)):
            for tile in range(wide // LANES):
                line = found[at : at + 1, tile * LANES : tile * LANES + LANES]
                first_part[level, tile, low:high, :] = jnp.broadcast_to(line, (high - low, LANES))


def stencil(centre, above, below, other, coef, ocean):
    wide = centre.shape[1]
    beside = (above + below) + (pltpu.roll(centre, 1, 1) + pltpu.roll(centre, wide - 1, 1))
    return ocean * (coef * centre - beside - 0.5 * other)


SEGMENTS = ((TOP - HALO, TOP, 0), (TOP, 40, 1), (40, 72, 2), (72, 72 + HALO, 3))


def image_kernel(
    obs, kap, bits, land, from_prev, from_next, gathered, spread,
    signed, first_dir, image, first_image, sums_low, sums_high, totals,
    ocean, coef, jacobi, first_rhs,
    word_bits, direction, inner, first_direction, first_inner, probe_part, first_part,
):
    lat_at = lax.axis_index("lat")
    lat_count = lax.axis_size("lat")
    lon_rows, width = land.shape
    wide = width + LANES
    rows = ocean.shape[1]
    lane = iota((rows, LANES), 1)
    before = gathered[jnp.maximum(lat_at - 1, 0), 0:rows, :]
    after = gathered[jnp.minimum(lat_at + 1, lat_count - 1), 0:rows, :]
    take_before = (lane >= LANES - HALO) & (lat_at > 0)
    take_after = (lane < HALO) & (lat_at < lat_count - 1)

    def extended(at, field):
        left = pltpu.roll(before, (LANES - HALO - 6 * at - 3) % LANES, 1)
        right = pltpu.roll(after, -6 * at % LANES, 1) if at else after
        tile = jnp.where(take_before, left, jnp.where(take_after, right, 0.0))
        ends = jnp.zeros((TOP - HALO, width), F32)
        main = jnp.concatenate(
            [
                ends,
                from_prev[HALO * at : HALO * at + HALO, :],
                field,
                from_next[HALO * at : HALO * at + HALO, :],
                ends,
            ],
            axis=0,
        )
        return jnp.concatenate([main, tile], axis=1)

    fields = raw_fields(obs, kap, bits, land)
    wet = extended(8, fields[8])
    keep(ocean, wet)
    for level in range(2):
        value = extended(2 + level, fields[2 + level]) + 5.0
        keep(coef.at[level], value)
        keep(jacobi.at[level], wet / (value * value + 4.0))
        keep(first_rhs.at[level], wet * extended(level, fields[level]))
        for word in range(2):
            at = 4 + word * 2 + level
            keep(word_bits.at[word, level], extended(at, fields[at]).astype(jnp.int32))
    corrections(gathered, spread, probe_part, first_part)
    bit = jnp.left_shift(1, iota((8, wide), 0))
    zero = jnp.zeros((8, width), F32)

    gamma = (zero, zero)
    for low, high, column in SEGMENTS:
        own = column in (1, 2)

        def body(row, carry, column=column, own=own):
            sea = same_row(ocean, row, 0)
            carry = list(carry)
            for level in range(2):
                weight = same_row(jacobi.at[level], row, 0)
                for word in range(2):
                    held = same_row(word_bits.at[word, level], row, 0)
                    rhs = jnp.where((held & bit) != 0, sea, -sea)
                    at = column * 24 + word * 8
                    value = weight * rhs + sea * probe_part[level, at : at + 8, :]
                    direction[level, word, row - (TOP - HALO)] = value
                    if own:
                        both = (rhs * value)[:, :width]
                        signed[level, word, row - TOP] = both
                        carry[word] = carry[word] + both
            return tuple(carry)

        gamma = lax.fori_loop(low, high, body, gamma)
    first_gamma = zero
    for step in range(14):
        row = TOP - HALO + step
        sea = same_row(ocean, row, 8)
        for level in range(2):
            rhs = same_row(first_rhs.at[level], row, 8)
            value = same_row(jacobi.at[level], row, 8) * rhs + sea * same_row(first_part.at[level], row, 8)
            first_direction[level, step] = value
            if HALO <= step < HALO + 8:
                first_dir[level, step - HALO] = value[:, :width]
                first_gamma = first_gamma + (rhs * value)[:, :width]

    def apply_first(row, carry, own):
        sea = same_row(ocean, row, 0)
        carry = list(carry)
        for level in range(2):
            scale = same_row(coef.at[level], row, 0)
            for word in range(2):
                at = row - (TOP - HALO)
                value = stencil(
                    direction[level, word, at],
                    direction[level, word, at - 1],
                    direction[level, word, at + 1],
                    direction[1 - level, word, at],
                    scale,
                    sea,
                )
                inner[level, word, at] = value
                if own:
                    part = value[:, :width]
                    carry[word] = carry[word] + part * part
        return tuple(carry)

    norm = (zero, zero)
    norm = lax.fori_loop(TOP - 2, TOP, functools.partial(apply_first, own=False), norm)
    norm = lax.fori_loop(TOP, TOP + lon_rows, functools.partial(apply_first, own=True), norm)
    norm = lax.fori_loop(
        TOP + lon_rows, TOP + lon_rows + 2, functools.partial(apply_first, own=False), norm
    )
    first_norm = zero
    for step in range(1, 13):
        row = TOP - HALO + step
        sea = same_row(ocean, row, 8)
        for level in range(2):
            value = stencil(
                first_direction[level, step],
                first_direction[level, step - 1],
                first_direction[level, step + 1],
                first_direction[1 - level, step],
                same_row(coef.at[level], row, 8),
                sea,
            )
            first_inner[level, step] = value
            if HALO <= step < HALO + 8:
                part = value[:, :width]
                first_norm = first_norm + part * part

    def apply_second(row, carry, own):
        sea = same_row(ocean, row, 0)
        carry = list(carry)
        for level in range(2):
            scale = same_row(coef.at[level], row, 0)
            for word in range(2):
                at = row - (TOP - HALO)
                value = stencil(
                    inner[level, word, at],
                    inner[level, word, at - 1],
                    inner[level, word, at + 1],
                    inner[1 - level, word, at],
                    scale,
                    sea,
                )
                image[level, word, row - (TOP - 1)] = value
                if own:
                    carry[level * 2 + word] = carry[level * 2 + word] + value[:, :width]
        return tuple(carry)

    none = (zero,) * 4
    lax.fori_loop(TOP - 1, TOP, functools.partial(apply_second, own=False), none)
    sums = {}
    for column in range(2):
        low = TOP + column * BLK
        got = lax.fori_loop(low, low + BLK, functools.partial(apply_second, own=True), none)
        for level in range(2):
            for word in range(2):
                sums[column, word, level] = got[level * 2 + word]
    lax.fori_loop(TOP + lon_rows, TOP + lon_rows + 1, functools.partial(apply_second, own=False), none)
    first_sum = [zero, zero]
    for step in range(2, 12):
        row = TOP - HALO + step
        sea = same_row(ocean, row, 8)
        for level in range(2):
            value = stencil(
                first_inner[level, step],
                first_inner[level, step - 1],
                first_inner[level, step + 1],
                first_inner[1 - level, step],
                same_row(coef.at[level], row, 8),
                sea,
            )
            first_image[level, step - 2] = value
            if HALO <= step < HALO + 8:
                first_sum[level] = first_sum[level] + value[:, :width]
    for level in range(2):
        for column in range(2):
            half = first_sum[level][column * 4 : column * 4 + 4]
            sums[column, 2, level] = first_row(jnp.sum(half, axis=0, keepdims=True))
    stacked = [
        jnp.concatenate([sums[column, group, level] for column in range(2) for group in range(3)], axis=0)
        for level in range(2)
    ]
    found = block_sums(lat_at, stacked)
    sums_low[...] = found[:24]
    sums_high[...] = found[24:]
    for at, value in enumerate((gamma[0], gamma[1], first_gamma, norm[0], norm[1], first_norm)):
        totals[at] = value[:, :LANES] + value[:, LANES:]


def second_kernel(
    gathered, spread, image, first_image, totals, ocean, coef, jacobi,
    packed, second, first_second,
    held, first_held, probe_part, first_part,
):
    width = second.shape[-1]
    lon_rows = second.shape[2]
    corrections(gathered, spread, probe_part, first_part)
    zero = jnp.zeros((8, width), F32)
    cross = (zero, zero)
    for low, high, column in ((TOP - 1, TOP, 0), (TOP, 40, 1), (40, 72, 2), (72, 73, 3)):
        own = column in (1, 2)

        def body(row, carry, column=column, own=own):
            sea = same_row(ocean, row, 0)
            carry = list(carry)
            for level in range(2):
                weight = same_row(jacobi.at[level], row, 0)
                for word in range(2):
                    at = column * 24 + word * 8
                    source = image[level, word, row - (TOP - 1)]
                    value = weight * source + sea * probe_part[level, at : at + 8, :]
                    held[level, word, row - (TOP - 1)] = value
                    if own:
                        second[level, word, row - TOP] = value[:, :width]
                        carry[word] = carry[word] + (value * source)[:, :width]
            return tuple(carry)

        cross = lax.fori_loop(low, high, body, cross)
    first_cross = zero
    for step in range(10):
        row = TOP - 1 + step
        sea = same_row(ocean, row, 8)
        for level in range(2):
            source = first_image[level, step]
            value = same_row(jacobi.at[level], row, 8) * source + sea * same_row(
                first_part.at[level], row, 8
            )
            first_held[level, step] = value
            if 1 <= step < 9:
                first_second[level, step - 1] = value[:, :width]
                first_cross = first_cross + (value * source)[:, :width]

    def apply(row, carry):
        sea = same_row(ocean, row, 0)
        carry = list(carry)
        for level in range(2):
            scale = same_row(coef.at[level], row, 0)
            for word in range(2):
                at = row - (TOP - 1)
                value = stencil(
                    held[level, word, at],
                    held[level, word, at - 1],
                    held[level, word, at + 1],
                    held[1 - level, word, at],
                    scale,
                    sea,
                )[:, :width]
                carry[word] = carry[word] + value * value
        return tuple(carry)

    norm = lax.fori_loop(TOP, TOP + lon_rows, apply, (zero, zero))
    first_norm = zero
    for step in range(1, 9):
        row = TOP - 1 + step
        sea = same_row(ocean, row, 8)
        for level in range(2):
            value = stencil(
                first_held[level, step],
                first_held[level, step - 1],
                first_held[level, step + 1],
                first_held[1 - level, step],
                same_row(coef.at[level], row, 8),
                sea,
            )[:, :width]
            first_norm = first_norm + value * value
    found = [totals[at] for at in range(6)] + [
        value[:, :LANES] + value[:, LANES:]
        for value in (cross[0], cross[1], first_cross, norm[0], norm[1], first_norm)
    ]
    lane = iota((8, LANES), 1)
    probe = iota((8, LANES), 0)
    out = jnp.zeros((8, LANES), F32)
    for kind in range(4):
        for group in range(3):
            total = jnp.broadcast_to(
                jnp.sum(found[kind * 3 + group], axis=1, keepdims=True), (8, LANES)
            )
            place = lane == (64 + kind if group == 2 else (kind * 2 + group) * 8 + probe)
            out = out + jnp.where(place, total, 0.0)
    packed[...] = jnp.broadcast_to(jnp.sum(out, axis=0, keepdims=True), packed.shape)


def sign_kernel(second, bits, land, out, ocean):
    lon_rows, width = land.shape
    keep(ocean, land[...].astype(F32))
    bit = jnp.left_shift(1, iota((8, width), 0))

    def body(row, carry):
        sea = same_row(ocean, row, 0)
        for level in range(2):
            for word in range(2):
                held = row_of(bits.at[word, level], row)
                out[level, word, row] = jnp.where((held & bit) != 0, sea, -sea) * second[level, word, row]
        return carry

    lax.fori_loop(0, lon_rows, body, 0, unroll=2)


def finish_kernel(packed, signed, signed_second, first_dir, first_second, kap, solution, diagonal, residual, natural):
    width = kap.shape[-1]
    lon_rows = kap.shape[1]
    total = jnp.broadcast_to(jnp.sum(packed[...], axis=0, keepdims=True), (8, LANES))
    lane = iota((8, LANES), 1)
    probe = iota((8, LANES), 0)

    def weights(group):
        found = []
        for kind in range(4):
            place = lane == (64 + kind if group == 2 else (kind * 2 + group) * 8 + probe)
            found.append(
                jnp.broadcast_to(
                    jnp.sum(jnp.where(place, total, 0.0), axis=1, keepdims=True), (8, LANES)
                )
            )
        gamma, norm, cross, second = found
        ratio = cross / norm
        rest = second - ratio * cross
        alive = rest > 0.0
        later = jnp.where(alive, (norm - ratio * gamma) / jnp.where(alive, rest, 1.0), 0.0)
        earlier = gamma / norm - later * ratio
        return (
            jnp.concatenate([earlier] * (width // LANES), axis=1),
            jnp.concatenate([later] * (width // LANES), axis=1),
        )

    low, high, first = weights(0), weights(1), weights(2)

    def body(row, carry):
        for level in range(2):
            value = (
                low[0] * signed[level, 0, row]
                + low[1] * signed_second[level, 0, row]
                + high[0] * signed[level, 1, row]
                + high[1] * signed_second[level, 1, row]
            )
            diagonal[level, pl.ds(row, 1), :] = jnp.sum(value, axis=0, keepdims=True) / PROBES
        return carry

    lax.fori_loop(0, lon_rows, body, 0, unroll=4)
    for level in range(2):
        for step in range(8):
            value = first[0] * first_dir[level, step] + first[1] * first_second[level, step]
            for tile in range(width // LANES):
                natural[level, tile, pl.ds(step, 8, stride=8), :] = value[:, tile * LANES : tile * LANES + LANES]
        solution[level] = jnp.concatenate([natural[level, tile] for tile in range(width // LANES)], axis=1)
        coef = kap[level] + 5.0
        bound = 0.5 / (coef * coef + 4.0)
        residual[level] = solution[level] / jnp.maximum(diagonal[level], bound)


def call(kernel, outs, scratch=(), limit=24, cost=None):
    return functools.partial(
        _run, kernel, outs, scratch, limit, cost
    )


def _run(kernel, outs, scratch, limit, cost, *args):
    return pl.pallas_call(
        kernel,
        out_shape=outs,
        in_specs=vmem(len(args)),
        out_specs=tuple(vmem(len(outs))),
        scratch_shapes=list(scratch),
        compiler_params=pltpu.CompilerParams(vmem_limit_bytes=limit << 20),
        cost_estimate=cost,
    )(*args)


def per_device(observed, kappa_squared, probe_bits, land_sea, coarse_block_inverse):
    lon_rows, width = land_sea.shape
    wide = width + LANES
    rows = lon_rows + 2 * TOP
    lon_count = lax.axis_size("lon")
    lat_count = lax.axis_size("lat")
    onward = [(i, (i + 1) % lon_count) for i in range(lon_count)]
    back = [((i + 1) % lon_count, i) for i in range(lon_count)]
    raw = (observed, kappa_squared, probe_bits, land_sea)

    to_prev, to_next, own = call(
        prepare_kernel,
        (shape(48, width), shape(48, width), shape(96, LANES)),
        [pltpu.VMEM((width // LANES, lon_rows, LANES), F32)],
    )(*raw)
    from_prev = lax.ppermute(to_next, "lon", onward)
    from_next = lax.ppermute(to_prev, "lon", back)
    (spread,) = call(spread_kernel, (shape(2, LANES, wide),))(coarse_block_inverse)
    (merged,) = call(merge_kernel, (shape(96, LANES),))(own, from_prev, from_next)
    gathered = lax.all_gather(merged, "lat")
    probe_parts = pltpu.VMEM((2, 96, wide), F32)
    tiles = wide // LANES
    first_parts = pltpu.VMEM((2, tiles, rows, LANES), F32)
    (
        signed, first_dir, image, first_image, sums_low, sums_high, totals,
        ocean, coef, jacobi, _,
    ) = call(
        image_kernel,
        (
            shape(2, 2, lon_rows, 8, width),
            shape(2, 8, 8, width),
            shape(2, 2, lon_rows + 2, 8, wide),
            shape(2, 10, 8, wide),
            shape(24, LANES),
            shape(24, LANES),
            shape(6, 8, LANES),
            shape(tiles, rows, LANES),
            shape(2, tiles, rows, LANES),
            shape(2, tiles, rows, LANES),
            shape(2, tiles, rows, LANES),
        ),
        [
            pltpu.VMEM((2, 2, tiles, rows, LANES), jnp.int32),
            pltpu.VMEM((2, 2, lon_rows + 2 * HALO, 8, wide), F32),
            pltpu.VMEM((2, 2, lon_rows + 2 * HALO, 8, wide), F32),
            pltpu.VMEM((2, 14, 8, wide), F32),
            pltpu.VMEM((2, 14, 8, wide), F32),
            probe_parts,
            first_parts,
        ],
    )(*raw, from_prev, from_next, gathered, spread)

    sums_prev = lax.ppermute(sums_high, "lon", onward)
    sums_next = lax.ppermute(sums_low, "lon", back)
    sums = lax.all_gather(jnp.concatenate([sums_prev, sums_low, sums_high, sums_next], axis=0), "lat")
    packed, second, first_second = call(
        second_kernel,
        (
            shape(lon_count * lat_count, LANES),
            shape(2, 2, lon_rows, 8, width),
            shape(2, 8, 8, width),
        ),
        [
            pltpu.VMEM((2, 2, lon_rows + 2, 8, wide), F32),
            pltpu.VMEM((2, 10, 8, wide), F32),
            probe_parts,
            first_parts,
        ],
    )(sums, spread, image, first_image, totals, ocean, coef, jacobi)
    everyone = lax.all_to_all(packed, ("lon", "lat"), 0, 0)
    (signed_second,) = call(
        sign_kernel,
        (shape(2, 2, lon_rows, 8, width),),
        [pltpu.VMEM((width // LANES, lon_rows, LANES), F32)],
    )(second, probe_bits, land_sea)
    return tuple(
        call(
            finish_kernel,
            (shape(2, lon_rows, width),) * 3,
            [pltpu.VMEM((2, width // LANES, lon_rows, LANES), F32)],
        )(
            everyone, signed, signed_second, first_dir, first_second, kappa_squared
        )
    )


def solution(mesh):
    placed = (
        P(None, "lon", "lat"),
        P(None, "lon", "lat"),
        P(None, None, "lon", "lat"),
        P("lon", "lat"),
        P(),
    )
    return jax.shard_map(
        per_device,
        mesh=mesh,
        in_specs=placed,
        out_specs=(P(None, "lon", "lat"), P(None, "lon", "lat"), P(None, "lon", "lat")),
        check_vma=False,
    )
```

```python
import functools

import jax
import jax.numpy as jnp
from jax import lax
from jax.experimental import pallas as pl
from jax.experimental.pallas import tpu as pltpu
from jax.sharding import PartitionSpec as P

BLK = 32
PROBES = 16
HALO = 3
TOP = 8
LANES = 128
EXACT = lax.Precision.HIGHEST
F32 = jnp.float32


def vmem(count):
    return [pl.BlockSpec(memory_space=pltpu.VMEM)] * count


def shape(*dims):
    return jax.ShapeDtypeStruct(dims, F32)


def iota(dims, axis):
    return lax.broadcasted_iota(jnp.int32, dims, axis)


def same_row(ref, row, stride):
    found = []
    for tile in range(ref.shape[0]):
        if stride == 0:
            found.append(ref[tile, pl.ds(row, 8, stride=0), :])
        else:
            found.append(ref[tile, pl.ds(row, 8, stride=stride), :])
    return jnp.concatenate(found, axis=1)


def keep(ref, value):
    for tile in range(ref.shape[0]):
        ref[tile] = value[:, tile * LANES : tile * LANES + LANES]


def row_of(ref, row):
    return jnp.broadcast_to(ref[pl.ds(row, 1), :], (8, ref.shape[1]))


def fetch(sources, targets, sems):
    copies = [
        pltpu.make_async_copy(source, target, sems.at[at])
        for at, (source, target) in enumerate(zip(sources, targets))
    ]
    for copy in copies:
        copy.start()
    for copy in copies:
        copy.wait()


def block_lanes(lat_at, level, width):
    source = iota((width, LANES), 0)
    lane = iota((width, LANES), 1)
    return jnp.where(lane == 64 + 16 * lat_at + 8 * level + source // BLK, 1.0, 0.0).astype(F32)


def block_sums(lat_at, rows):
    total = None
    for level in range(2):
        part = jnp.dot(
            rows[level],
            block_lanes(lat_at, level, rows[level].shape[1]),
            precision=EXACT,
            preferred_element_type=F32,
        )
        total = part if total is None else total + part
    return total


def first_row(row):
    return jnp.where(iota((8, row.shape[1]), 0) == 0, jnp.broadcast_to(row, (8, row.shape[1])), 0.0)


def raw_fields(obs, kap, bits, land):
    return (
        [obs[level] for level in range(2)]
        + [kap[level] for level in range(2)]
        + [bits[word, level].astype(F32) for word in range(2) for level in range(2)]
        + [land[...].astype(F32)]
    )


def prepare_kernel(
    obs_in, kap_in, bits_in, land_in, to_odd, to_even, own,
    obs, kap, bits, land, ocean, sems,
):
    fetch((obs_in, kap_in, bits_in, land_in), (obs, kap, bits, land), sems)
    lat_at = lax.axis_index("lat")
    even = lax.rem(lax.axis_index("lon"), 2) == 0
    lon_rows, width = land.shape
    fields = raw_fields(obs, kap, bits, land)
    lane = iota((lon_rows, LANES), 1)
    edges = jnp.zeros((lon_rows, LANES), F32)
    for at, field in enumerate(fields):
        first, last = field[:HALO], field[lon_rows - HALO :]
        here = slice(HALO * at, HALO * at + HALO)
        to_odd[here, :] = jnp.where(even, first, last)
        to_even[here, :] = jnp.where(even, last, first)
        low = pltpu.roll(field[:, :LANES], 6 * at, 1) if at else field[:, :LANES]
        high = pltpu.roll(field[:, width - LANES :], (6 * at + 6) % LANES, 1)
        edges = jnp.where((lane >= 6 * at) & (lane < 6 * at + 3), low, edges)
        edges = jnp.where((lane >= 6 * at + 3) & (lane < 6 * at + 6), high, edges)
    to_odd[27:30, :LANES] = jnp.where(even, edges[:HALO], edges[lon_rows - HALO :])
    to_even[27:30, :LANES] = jnp.where(even, edges[lon_rows - HALO :], edges[:HALO])
    keep(ocean, fields[8])
    bit = jnp.left_shift(1, iota((8, width), 0))
    zero = jnp.zeros((8, width), F32)
    sums = {}
    for column in range(2):
        for word in range(2):
            for level in range(2):
                sums[column, word, level] = zero

        def body(row, carry):
            wet = same_row(ocean, row, 0)
            out = []
            for word in range(2):
                for level in range(2):
                    held = row_of(bits.at[word, level], row)
                    out.append(carry[word * 2 + level] + jnp.where((held & bit) != 0, wet, -wet))
            return tuple(out)

        got = lax.fori_loop(column * BLK, column * BLK + BLK, body, (zero,) * 4, unroll=BLK)
        for word in range(2):
            for level in range(2):
                sums[column, word, level] = got[word * 2 + level]
        for level in range(2):
            held = slice(column * BLK, column * BLK + BLK)
            sums[column, 2, level] = first_row(
                jnp.sum(fields[8][held] * fields[level][held], axis=0, keepdims=True)
            )
    rows = [
        jnp.concatenate([sums[column, group, level] for column in range(2) for group in range(3)], axis=0)
        for level in range(2)
    ]
    found = block_sums(lat_at, rows)
    own[...] = jnp.zeros(own.shape, F32)
    own[TOP : TOP + lon_rows, :] = edges
    own[24:72, :] = own[24:72, :] + found
    first, last = found[:24], found[24:]
    for target, part in (
        (to_odd, jnp.where(even, first, last)),
        (to_even, jnp.where(even, last, first)),
    ):
        target[32:40, :LANES] = part[:8]
        target[32:40, LANES : 2 * LANES] = part[8:16]
        target[40:48, :LANES] = part[16:24]


def merge_kernel(own, from_odd, from_even, out):
    even = lax.rem(lax.axis_index("lon"), 2) == 0
    odd_part, even_part = from_odd[...], from_even[...]
    prev = jnp.where(even, odd_part, even_part)
    later = jnp.where(even, even_part, odd_part)
    out[...] = own[...]
    for source, row, at in ((prev, TOP - HALO, 0), (later, TOP + 64, 72)):
        out[row : row + HALO, :] = out[row : row + HALO, :] + source[27:30, :LANES]
        out[at : at + 8, :] = out[at : at + 8, :] + source[32:40, :LANES]
        out[at + 8 : at + 16, :] = out[at + 8 : at + 16, :] + source[32:40, LANES : 2 * LANES]
        out[at + 16 : at + 24, :] = out[at + 16 : at + 24, :] + source[40:48, :LANES]


def base_kernel(
    obs_in, kap_in, bits_in, land_in, coarse_in, spread, ocean, coef, jacobi, first_rhs, word_bits,
    obs, kap, bits, land, coarse, sems,
):
    fetch(
        (obs_in, kap_in, bits_in, land_in, coarse_in), (obs, kap, bits, land, coarse), sems
    )
    lat_at = lax.axis_index("lat")
    wide = spread.shape[2]
    width = wide - LANES
    per = width // BLK
    lane = iota((32, wide), 1)
    block = jnp.where(lane < width, lane // BLK, -1000)
    block = jnp.where((lane >= width) & (lane < width + HALO), per, block)
    block = jnp.where(lane >= wide - HALO, -1, block)
    chosen = jnp.where(iota((32, wide), 0) == block + per * lat_at, 1.0, 0.0).astype(F32)
    for level in range(2):
        spread[level, 0:64, :] = jnp.zeros((64, wide), F32)
        for other in range(2):
            part = lax.dot_general(
                coarse[level, :, other, :],
                chosen,
                (((0,), (0,)), ((), ())),
                precision=EXACT,
                preferred_element_type=F32,
            )
            for group in range(4):
                at = 64 + 16 * group + 8 * other
                spread[level, at : at + 8, :] = part[8 * group : 8 * group + 8]

    def place(ref, value):
        ends = jnp.zeros((TOP, LANES), value.dtype)
        for tile in range(width // LANES):
            ref[tile, 0:TOP] = ends
            ref[tile, TOP : TOP + land.shape[0]] = value[:, tile * LANES : tile * LANES + LANES]
            ref[tile, TOP + land.shape[0] :] = ends

    wet = land[...].astype(F32)
    place(ocean, wet)
    for level in range(2):
        value = kap[level] + 5.0
        place(coef.at[level], value)
        place(jacobi.at[level], wet / (value * value + 4.0))
        place(first_rhs.at[level], wet * obs[level])
        for word in range(2):
            place(word_bits.at[word, level], bits[word, level])


def corrections(gathered, spread, probe_part, even=None):
    total = gathered[0] + gathered[1] + gathered[2] + gathered[3]
    total = jnp.where(iota(total.shape, 1) >= 64, total, 0.0)
    if even is not None:
        first, last = total[:24], total[72:]
        total = jnp.concatenate(
            [jnp.where(even, first, last), total[24:72], jnp.where(even, last, first)], axis=0
        )
    for level in range(2):
        probe_part[level] = jnp.dot(total, spread[level], precision=EXACT, preferred_element_type=F32)


def first_corrections(probe_part, first_part):
    for level in range(2):
        for low, high, at in ((TOP - HALO, TOP, 16), (TOP, 40, 40), (40, 72, 64), (72, 72 + HALO, 88)):
            for tile in range(first_part.shape[1]):
                line = probe_part[level, at : at + 1, tile * LANES : tile * LANES + LANES]
                first_part[level, tile, low:high, :] = jnp.broadcast_to(line, (high - low, LANES))


def stencil(centre, above, below, other, coef, ocean):
    wide = centre.shape[1]
    beside = (above + below) + (pltpu.roll(centre, 1, 1) + pltpu.roll(centre, wide - 1, 1))
    return ocean * (coef * centre - beside - 0.5 * other)


SEGMENTS = ((TOP - HALO, TOP, 0), (TOP, 40, 1), (40, 72, 2), (72, 72 + HALO, 3))


def apply_rows(load, coef, ocean, begin, count, emit):
    for word in range(2):
        held = {}
        for step in range(2):
            for level in range(2):
                held[level, step] = load(level, word, begin - 1 + step)
        for step in range(1, count + 1):
            for level in range(2):
                held[level, step + 1] = load(level, word, begin + step)
            row = begin + step - 1
            sea = same_row(ocean, row, 0)
            for level in range(2):
                emit(
                    level,
                    word,
                    row,
                    stencil(
                        held[level, step],
                        held[level, step - 1],
                        held[level, step + 1],
                        held[1 - level, step],
                        same_row(coef.at[level], row, 0),
                        sea,
                    ),
                )


def image_kernel(
    base_ocean, base_coef, base_jacobi, base_first, base_bits,
    from_odd, from_even, gathered, spread,
    image, first_image, to_odd, to_even, own_sums, row_sums, totals, own_part,
    ocean, coef, jacobi,
    first_rhs, word_bits, direction, inner, first_direction, first_inner, probe_part, first_part,
):
    lat_at = lax.axis_index("lat")
    even = lax.rem(lax.axis_index("lon"), 2) == 0
    lat_count = lax.axis_size("lat")
    tiles, rows, _ = ocean.shape
    width = (tiles - 1) * LANES
    wide = tiles * LANES
    lon_rows = rows - 2 * TOP
    lane = iota((rows, LANES), 1)
    before = gathered[jnp.maximum(lat_at - 1, 0), 0:rows, :]
    after = gathered[jnp.minimum(lat_at + 1, lat_count - 1), 0:rows, :]
    take_before = (lane >= LANES - HALO) & (lat_at > 0)
    take_after = (lane < HALO) & (lat_at < lat_count - 1)
    odd_part, even_part = from_odd[0:32, :], from_even[0:32, :]
    prev = jnp.where(even, odd_part, even_part)
    later = jnp.where(even, even_part, odd_part)

    def outside(at):
        left = pltpu.roll(before, (LANES - HALO - 6 * at - 3) % LANES, 1)
        right = pltpu.roll(after, -6 * at % LANES, 1) if at else after
        tile = jnp.where(take_before, left, jnp.where(take_after, right, 0.0))
        here = slice(HALO * at, HALO * at + HALO)
        return prev[here], later[here], tile

    def fill(ref, base, parts):
        for tile in range(tiles - 1):
            lanes = slice(tile * LANES, tile * LANES + LANES)
            ref[tile] = base[tile]
            ref[tile, TOP - HALO : TOP] = parts[0][:, lanes]
            ref[tile, TOP + lon_rows : TOP + lon_rows + HALO] = parts[1][:, lanes]
        ref[tiles - 1] = parts[2]

    wet = outside(8)
    fill(ocean, base_ocean, wet)
    for level in range(2):
        value = [part + 5.0 for part in outside(2 + level)]
        fill(coef.at[level], base_coef.at[level], value)
        fill(
            jacobi.at[level],
            base_jacobi.at[level],
            [sea / (part * part + 4.0) for sea, part in zip(wet, value)],
        )
        fill(
            first_rhs.at[level],
            base_first.at[level],
            [sea * part for sea, part in zip(wet, outside(level))],
        )
        for word in range(2):
            fill(
                word_bits.at[word, level],
                base_bits.at[word, level],
                [part.astype(jnp.int32) for part in outside(4 + word * 2 + level)],
            )
    corrections(gathered, spread, probe_part)
    first_corrections(probe_part, first_part)
    own_part[...] = probe_part[:, 24:72, :width]
    bit = jnp.left_shift(1, iota((8, wide), 0))
    zero = jnp.zeros((8, width), F32)

    gamma = (zero, zero)
    for low, high, column in SEGMENTS:
        own = column in (1, 2)

        def body(row, carry, column=column, own=own):
            sea = same_row(ocean, row, 0)
            carry = list(carry)
            for level in range(2):
                weight = same_row(jacobi.at[level], row, 0)
                for word in range(2):
                    held = same_row(word_bits.at[word, level], row, 0)
                    rhs = jnp.where((held & bit) != 0, sea, -sea)
                    at = column * 24 + word * 8
                    value = weight * rhs + sea * probe_part[level, at : at + 8, :]
                    direction[level, word, row - (TOP - HALO)] = value
                    if own:
                        carry[word] = carry[word] + (rhs * value)[:, :width]
            return tuple(carry)

        gamma = lax.fori_loop(low, high, body, gamma, unroll=16 if own else HALO)
    first_gamma = zero
    for step in range(14):
        row = TOP - HALO + step
        sea = same_row(ocean, row, 8)
        for level in range(2):
            rhs = same_row(first_rhs.at[level], row, 8)
            value = same_row(jacobi.at[level], row, 8) * rhs + sea * same_row(first_part.at[level], row, 8)
            first_direction[level, step] = value
            if HALO <= step < HALO + 8:
                first_gamma = first_gamma + (rhs * value)[:, :width]

    def load_direction(level, word, row):
        return direction[level, word, row - (TOP - HALO)]

    def first_body(column, carry, low, count, own):
        carry = list(carry)

        def emit(level, word, row, value):
            inner[level, word, row - (TOP - HALO)] = value
            if own:
                part = value[:, :width]
                carry[word] = carry[word] + part * part

        apply_rows(load_direction, coef, ocean, low + column * count, count, emit)
        return tuple(carry)

    norm = first_body(0, (zero, zero), TOP - 2, 2, False)
    norm = lax.fori_loop(
        0, 2, functools.partial(first_body, low=TOP, count=BLK, own=True), norm
    )
    norm = first_body(0, norm, TOP + lon_rows, 2, False)
    first_norm = zero
    for step in range(1, 13):
        row = TOP - HALO + step
        sea = same_row(ocean, row, 8)
        for level in range(2):
            value = stencil(
                first_direction[level, step],
                first_direction[level, step - 1],
                first_direction[level, step + 1],
                first_direction[1 - level, step],
                same_row(coef.at[level], row, 8),
                sea,
            )
            first_inner[level, step] = value
            if HALO <= step < HALO + 8:
                part = value[:, :width]
                first_norm = first_norm + part * part

    def load_inner(level, word, row):
        return inner[level, word, row - (TOP - HALO)]

    def second_body(column, carry, low, count, own):
        added = {}

        def emit(level, word, row, value):
            image[level, word, row - (TOP - 1)] = value
            if own:
                part = value[:, :width]
                added[level, word] = added[level, word] + part if (level, word) in added else part

        apply_rows(load_inner, coef, ocean, low + column * count, count, emit)
        if own:
            for level in range(2):
                for word in range(2):
                    at = pl.multiple_of(column * 24, 8) + word * 8
                    row_sums[level, pl.ds(at, 8), :] = added[level, word]
        return carry

    second_body(0, 0, TOP - 1, 1, False)
    lax.fori_loop(0, 2, functools.partial(second_body, low=TOP, count=BLK, own=True), 0)
    second_body(0, 0, TOP + lon_rows, 1, False)
    first_sum = [zero, zero]
    for step in range(2, 12):
        row = TOP - HALO + step
        sea = same_row(ocean, row, 8)
        for level in range(2):
            value = stencil(
                first_inner[level, step],
                first_inner[level, step - 1],
                first_inner[level, step + 1],
                first_inner[1 - level, step],
                same_row(coef.at[level], row, 8),
                sea,
            )
            first_image[level, step - 2] = value
            if HALO <= step < HALO + 8:
                first_sum[level] = first_sum[level] + value[:, :width]
    for level in range(2):
        for column in range(2):
            half = first_sum[level][column * 4 : column * 4 + 4]
            row_sums[level, column * 24 + 16 : column * 24 + 24, :] = first_row(
                jnp.sum(half, axis=0, keepdims=True)
            )
    found = block_sums(lat_at, [row_sums[level] for level in range(2)])
    own_sums[...] = found
    to_odd[...] = jnp.where(even, found[:24], found[24:])
    to_even[...] = jnp.where(even, found[24:], found[:24])
    for at, value in enumerate((gamma[0], gamma[1], first_gamma, norm[0], norm[1], first_norm)):
        totals[at] = value[:, :LANES] + value[:, LANES:]


BASIS = (0, 256, 272, 288, 304, 312, 344)
PAIRS = [(first, last) for first in range(4) for last in range(first, 4)]
EDGES = (0, 31, 32, 63)


def products_kernel(
    image, first_image, ocean, coef, jacobi, base_first, base_bits,
    linear, quadratic, edge_value, edge_field, totals, basis,
    field, edge, natural,
):
    tiles, rows, _ = ocean.shape
    width = (tiles - 1) * LANES
    lon_rows = rows - 2 * TOP
    groups = lon_rows // 8
    zero = jnp.zeros((8, width), F32)
    bit = jnp.left_shift(1, iota((8, width), 0))

    def own_rows(ref):
        return jnp.concatenate(
            [ref[tile, TOP : TOP + lon_rows] for tile in range(tiles - 1)], axis=1
        )

    def put(at, value):
        for group in range(groups):
            basis[at + group] = value[8 * group : 8 * group + 8]

    whole = jnp.concatenate([ocean[tile, TOP : TOP + lon_rows] for tile in range(tiles)], axis=1)
    sea = whole[:, :width]
    up = jnp.concatenate([ocean[tile, TOP - 1 : TOP - 1 + lon_rows] for tile in range(tiles - 1)], axis=1)
    down = jnp.concatenate([ocean[tile, TOP + 1 : TOP + 1 + lon_rows] for tile in range(tiles - 1)], axis=1)
    row = iota((lon_rows, width), 0)
    first = lax.rem(row, BLK) == 0
    last = lax.rem(row, BLK) == BLK - 1
    inside = jnp.where(first | last, 0.0, 1.0)
    vertical = jnp.where(first, 0.0, up) + jnp.where(last, 0.0, down)
    across = -sea * (jnp.where(first, up, 0.0) + jnp.where(last, down, 0.0))
    left = -sea * pltpu.roll(whole, 1, 1)[:, :width]
    right = -sea * pltpu.roll(whole, tiles * LANES - 1, 1)[:, :width]
    other = -0.5 * sea
    put(BASIS[4], sea)
    selves = []
    for level in range(2):
        scale = own_rows(coef.at[level])
        put(BASIS[3] + level * groups, 0.5 / (scale * scale + 4.0))
        put(BASIS[1] + level * groups, own_rows(jacobi.at[level]) * own_rows(base_first.at[level]))
        for word in range(2):
            put(
                BASIS[5] + (word * 2 + level) * groups,
                own_rows(base_bits.at[word, level]).astype(F32),
            )
        selves.append(sea * (scale * sea - vertical))
    for at, value in enumerate(selves + [left, right, other]):
        keep(field.at[at], value * inside)
        for place, line in enumerate(EDGES):
            edge_field[place, at : at + 1, :] = value[line : line + 1]
    for place, line in enumerate(EDGES):
        edge_field[place, 5:6, :] = across[line : line + 1]
        edge_field[place, 6:8, :] = jnp.zeros((2, width), F32)
    for level in range(2):
        terms = [selves[level] * inside, left * inside, right * inside, other * inside]
        for at, (one, two) in enumerate(PAIRS):
            product = terms[one] * terms[two]
            for column in range(2):
                quadratic[level, column, at : at + 1, :] = jnp.sum(
                    product[column * BLK : column * BLK + BLK], axis=0, keepdims=True
                )

    def load(level, word, at):
        return same_row(jacobi.at[level], at, 0) * image[level, word, at - (TOP - 1)]

    def body(column, carry):
        carry = list(carry)
        sums = {}

        def emit(level, word, at, value):
            line = at - TOP
            part = value[:, :width]
            carry[2 + word] = carry[2 + word] + part * part
            edge[level, word, line] = part
            for kind, which in enumerate((level, 2, 3, 4)):
                term = part * same_row(field.at[which], line, 0)
                key = level, word, kind
                sums[key] = sums[key] + term if key in sums else term
            source = image[level, word, at - (TOP - 1)][:, :width]
            weighted = same_row(jacobi.at[level], at, 0)[:, :width] * source
            carry[word] = carry[word] + weighted * source
            held = same_row(base_bits.at[word, level], at, 0)
            basis[(level * 2 + word) * lon_rows + line] = jnp.where(
                (held & bit) != 0, weighted, -weighted
            )

        apply_rows(load, coef, ocean, TOP + column * BLK, BLK, emit)
        for (level, word, kind), value in sums.items():
            linear[level, column, word, kind] = value
        return tuple(carry)

    crossed = lax.fori_loop(0, 2, body, (zero,) * 4)
    for place, line in enumerate(EDGES):
        for level in range(2):
            for word in range(2):
                edge_value[place, level, word] = edge[level, word, line]

    first_cross, first_norm = zero, zero
    held = {}
    for level in range(2):
        for step in range(10):
            held[level, step] = same_row(jacobi.at[level], TOP - 1 + step, 8) * first_image[level, step]
    for level in range(2):
        for step in range(8):
            for tile in range(tiles - 1):
                natural[level, tile, pl.ds(step, 8, stride=8), :] = held[level, step + 1][
                    :, tile * LANES : tile * LANES + LANES
                ]
        put(
            BASIS[2] + level * groups,
            jnp.concatenate([natural[level, tile] for tile in range(tiles - 1)], axis=1),
        )
        sums = [zero] * 4
        for step in range(1, 9):
            at = TOP - 1 + step
            value = stencil(
                held[level, step],
                held[level, step - 1],
                held[level, step + 1],
                held[1 - level, step],
                same_row(coef.at[level], at, 8),
                same_row(ocean, at, 8),
            )[:, :width]
            first_norm = first_norm + value * value
            first_cross = first_cross + (held[level, step] * first_image[level, step])[:, :width]
            for kind, which in enumerate((level, 2, 3, 4)):
                sums[kind] = sums[kind] + value * same_row(field.at[which], step - 1, 8)
            if step == 1:
                edge_value[0, level, 2] = first_row(value[0:1])
                edge_value[2, level, 2] = first_row(value[4:5])
            if step == 8:
                edge_value[1, level, 2] = first_row(value[3:4])
                edge_value[3, level, 2] = first_row(value[7:8])
        for kind in range(4):
            for column in range(2):
                half = sums[kind][column * 4 : column * 4 + 4]
                linear[level, column, 2, kind] = first_row(jnp.sum(half, axis=0, keepdims=True))
    for at, value in enumerate((crossed[0], crossed[1], first_cross, crossed[2], crossed[3], first_norm)):
        totals[at] = value[:, :LANES] + value[:, LANES:]


def norms_kernel(
    gathered, spread, row_sums, linear, quadratic, edge_value, edge_field, early, late,
    packed, own_part, probe_part,
):
    even = lax.rem(lax.axis_index("lon"), 2) == 0
    corrections(gathered, spread, probe_part, even)
    wide = probe_part.shape[2]
    width = wide - LANES
    own_part[...] = probe_part[:, 24:72, :width]
    found = [early[at] for at in range(6)] + [late[at] for at in range(6)]

    def wide_row(value):
        return jnp.broadcast_to(value, (8, width))

    def own(level, column, group):
        at = column * 24 + group * 8
        return probe_part[level, at : at + 8, :]

    for level in range(2):
        for column in range(2):
            pairs = {
                pair: wide_row(quadratic[level, column, at : at + 1, :]) for at, pair in enumerate(PAIRS)
            }
            for group in range(3):
                here = own(level, column + 1, group)
                terms = [
                    here[:, :width],
                    pltpu.roll(here, 1, 1)[:, :width],
                    pltpu.roll(here, wide - 1, 1)[:, :width],
                    own(1 - level, column + 1, group)[:, :width],
                ]
                at = column * 24 + group * 8
                cross = terms[0] * row_sums[level, at : at + 8, :]
                norm = jnp.zeros((8, width), F32)
                for one in range(4):
                    inside = terms[one] * pairs[one, one]
                    double = linear[level, column, group, one]
                    for two in range(one + 1, 4):
                        double = double + terms[two] * pairs[one, two]
                    norm = norm + terms[one] * (inside + 2.0 * double)
                for place in (2 * column, 2 * column + 1):
                    beyond = (0, 2, 1, 3)[place]
                    value = edge_value[place, level, group]
                    for kind, which in enumerate((level, 2, 3, 4)):
                        value = value + terms[kind] * wide_row(edge_field[place, which : which + 1, :])
                    value = value + own(level, beyond, group)[:, :width] * wide_row(
                        edge_field[place, 5:6, :]
                    )
                    norm = norm + (value * value)
                    mine = edge_value[place, level, group]
                    norm = norm - mine * mine
                found[6 + group] = found[6 + group] + cross[:, :LANES] + cross[:, LANES:]
                found[9 + group] = found[9 + group] + norm[:, :LANES] + norm[:, LANES:]
    lane = iota((8, LANES), 1)
    probe = iota((8, LANES), 0)
    out = jnp.zeros((8, LANES), F32)
    for kind in range(4):
        for group in range(3):
            total = jnp.broadcast_to(
                jnp.sum(found[kind * 3 + group], axis=1, keepdims=True), (8, LANES)
            )
            place = lane == (64 + kind if group == 2 else (kind * 2 + group) * 8 + probe)
            out = out + jnp.where(place, total, 0.0)
    packed[...] = jnp.broadcast_to(jnp.sum(out, axis=0, keepdims=True), packed.shape)


def finish_kernel(packed, early_part, later_part, basis, solution, diagonal, residual, ocean, bits, held, sems):
    _, lon_rows, width = solution.shape
    groups = lon_rows // 8
    total = jnp.broadcast_to(jnp.sum(packed[...], axis=0, keepdims=True), (8, LANES))
    lane = iota((8, LANES), 1)
    probe = iota((8, LANES), 0)

    def get(at):
        return jnp.concatenate([basis[at + group] for group in range(groups)], axis=0)

    def send(which, level):
        target = (solution, diagonal, residual)[which]
        copy = pltpu.make_async_copy(held.at[which, level], target.at[level], sems.at[which, level])
        copy.start()
        return copy

    def weights(group):
        found = []
        for kind in range(4):
            place = lane == (64 + kind if group == 2 else (kind * 2 + group) * 8 + probe)
            found.append(
                jnp.broadcast_to(
                    jnp.sum(jnp.where(place, total, 0.0), axis=1, keepdims=True), (8, LANES)
                )
            )
        gamma, norm, cross, second = found
        ratio = cross / norm
        rest = second - ratio * cross
        alive = rest > 0.0
        later = jnp.where(alive, (norm - ratio * gamma) / jnp.where(alive, rest, 1.0), 0.0)
        earlier = gamma / norm - later * ratio
        return (
            jnp.concatenate([earlier] * (width // LANES), axis=1),
            jnp.concatenate([later] * (width // LANES), axis=1),
        )

    wet = get(BASIS[4])
    keep(ocean, wet)
    for level in range(2):
        for word in range(2):
            bits[word, level] = get(BASIS[5] + (word * 2 + level) * groups).astype(jnp.int32)
    system = [weights(group) for group in range(3)]
    bit = jnp.left_shift(1, iota((8, width), 0))
    row = iota((lon_rows, width), 0)
    share = jnp.sum(system[0][0] + system[1][0], axis=0, keepdims=True)
    share = 2.0 * wet * jnp.broadcast_to(share, (lon_rows, width))
    earlier, later = system[2][0][0:1], system[2][1][0:1]
    copies = []
    for level in range(2):
        lines = [
            earlier * early_part[level, at : at + 1, :] + later * later_part[level, at : at + 1, :]
            for at in (16, 40)
        ]
        held[0, level] = (
            earlier * get(BASIS[1] + level * groups)
            + later * get(BASIS[2] + level * groups)
            + wet * jnp.where(row < BLK, lines[0], lines[1])
        )
        copies.append(send(0, level))
    for level in range(2):
        for column in range(2):
            coarse = []
            for word in range(2):
                at = column * 24 + word * 8
                coarse.append(
                    system[word][0] * early_part[level, at : at + 8, :]
                    + system[word][1] * later_part[level, at : at + 8, :]
                )

            def body(line, carry, coarse=coarse, level=level):
                signs, rest = None, None
                for word in range(2):
                    signed = jnp.where(
                        (row_of(bits.at[word, level], line) & bit) != 0, coarse[word], -coarse[word]
                    )
                    second = system[word][1] * basis[(level * 2 + word) * lon_rows + line]
                    signs = signed if signs is None else signs + signed
                    rest = second if rest is None else rest + second
                whole = same_row(ocean, line, 0) * signs + rest
                held[1, level, pl.ds(line, 1), :] = jnp.sum(whole, axis=0, keepdims=True)
                return carry

            lax.fori_loop(column * BLK, column * BLK + BLK, body, 0, unroll=BLK)
        bound = get(BASIS[3] + level * groups)
        spread = (held[1, level] + share * bound) / PROBES
        held[1, level] = spread
        copies.append(send(1, level))
        held[2, level] = held[0, level] / jnp.maximum(spread, bound)
        copies.append(send(2, level))
    for copy in copies:
        copy.wait()


def call(kernel, outs, scratch=(), outside=0):
    return functools.partial(_run, kernel, outs, scratch, outside)


def _run(kernel, outs, scratch, outside, *args):
    held = [pltpu.with_memory_space_constraint(array, pltpu.HBM) for array in args[:outside]]
    return pl.pallas_call(
        kernel,
        out_shape=outs,
        in_specs=[pl.BlockSpec(memory_space=pltpu.HBM)] * outside + vmem(len(args) - outside),
        out_specs=tuple(vmem(len(outs))),
        scratch_shapes=list(scratch),
        compiler_params=pltpu.CompilerParams(vmem_limit_bytes=24 << 20),
    )(*held, *args[outside:])


def per_device(observed, kappa_squared, probe_bits, land_sea, coarse_block_inverse):
    lon_rows, width = land_sea.shape
    wide = width + LANES
    tiles = wide // LANES
    rows = lon_rows + 2 * TOP
    lon_count = lax.axis_size("lon")
    lat_count = lax.axis_size("lat")
    evens = [(i, i + 1 - 2 * (i % 2)) for i in range(lon_count)]
    odds = [(i, (i - 1 + 2 * (i % 2)) % lon_count) for i in range(lon_count)]
    raw = (observed, kappa_squared, probe_bits, land_sea)
    inside = [pltpu.VMEM(array.shape, array.dtype) for array in raw]
    sems = pltpu.SemaphoreType.DMA((4,))

    to_odd, to_even, own = call(
        prepare_kernel,
        (shape(48, width), shape(48, width), shape(96, LANES)),
        [*inside, pltpu.VMEM((width // LANES, lon_rows, LANES), F32), sems],
        4,
    )(*raw)
    from_odd = lax.ppermute(to_odd, "lon", odds)
    from_even = lax.ppermute(to_even, "lon", evens)
    natural = (tiles - 1, rows, LANES)
    spread, *base = call(
        base_kernel,
        (
            shape(2, LANES, wide),
            shape(*natural),
            shape(2, *natural),
            shape(2, *natural),
            shape(2, *natural),
            jax.ShapeDtypeStruct((2, 2, *natural), jnp.int32),
        ),
        [
            *inside,
            pltpu.VMEM(coarse_block_inverse.shape, F32),
            pltpu.SemaphoreType.DMA((5,)),
        ],
        5,
    )(*raw, coarse_block_inverse)
    (merged,) = call(merge_kernel, (shape(96, LANES),))(own, from_odd, from_even)
    gathered = lax.all_gather(merged, "lat")
    probe_parts = pltpu.VMEM((2, 96, wide), F32)
    first_parts = pltpu.VMEM((2, tiles, rows, LANES), F32)
    image, first_image, to_odd, to_even, own_sums, row_sums, early, own_part, ocean, coef, jacobi = call(
        image_kernel,
        (
            shape(2, 2, lon_rows + 2, 8, wide),
            shape(2, 10, 8, wide),
            shape(24, LANES),
            shape(24, LANES),
            shape(48, LANES),
            shape(2, 48, width),
            shape(6, 8, LANES),
            shape(2, 48, width),
            shape(tiles, rows, LANES),
            shape(2, tiles, rows, LANES),
            shape(2, tiles, rows, LANES),
        ),
        [
            first_parts,
            pltpu.VMEM((2, 2, tiles, rows, LANES), jnp.int32),
            pltpu.VMEM((2, 2, lon_rows + 2 * HALO, 8, wide), F32),
            pltpu.VMEM((2, 2, lon_rows + 2 * HALO, 8, wide), F32),
            pltpu.VMEM((2, 14, 8, wide), F32),
            pltpu.VMEM((2, 14, 8, wide), F32),
            probe_parts,
            first_parts,
        ],
    )(*base, from_odd, from_even, gathered, spread)

    sums_odd = lax.ppermute(to_odd, "lon", odds)
    sums_even = lax.ppermute(to_even, "lon", evens)
    blocks = width // LANES
    linear, quadratic, edge_value, edge_field, late, basis = call(
        products_kernel,
        (
            shape(2, 2, 3, 4, 8, width),
            shape(2, 2, 16, width),
            shape(4, 2, 3, 8, width),
            shape(4, 8, width),
            shape(6, 8, LANES),
            shape(BASIS[-1], 8, width),
        ),
        [
            pltpu.VMEM((5, blocks, lon_rows, LANES), F32),
            pltpu.VMEM((2, 2, lon_rows, 8, width), F32),
            pltpu.VMEM((2, blocks, lon_rows, LANES), F32),
        ],
    )(image, first_image, ocean, coef, jacobi, base[3], base[4])
    sums = lax.all_gather(jnp.concatenate([sums_odd, own_sums, sums_even], axis=0), "lat")
    packed, later_part = call(
        norms_kernel, (shape(lon_count * lat_count, LANES), shape(2, 48, width)), [probe_parts]
    )(
        sums, spread, row_sums, linear, quadratic, edge_value, edge_field, early, late
    )
    everyone = lax.all_to_all(packed, ("lon", "lat"), 0, 0)
    return tuple(
        pl.pallas_call(
            finish_kernel,
            out_shape=(shape(2, lon_rows, width),) * 3,
            in_specs=vmem(4),
            out_specs=tuple([pl.BlockSpec(memory_space=pltpu.HBM)] * 3),
            scratch_shapes=[
                pltpu.VMEM((blocks, lon_rows, LANES), F32),
                pltpu.VMEM((2, 2, lon_rows, width), jnp.int32),
                pltpu.VMEM((3, 2, lon_rows, width), F32),
                pltpu.SemaphoreType.DMA((3, 2)),
            ],
            compiler_params=pltpu.CompilerParams(vmem_limit_bytes=24 << 20),
        )(everyone, own_part, later_part, basis)
    )


def solution(mesh):
    placed = (
        P(None, "lon", "lat"),
        P(None, "lon", "lat"),
        P(None, None, "lon", "lat"),
        P("lon", "lat"),
        P(),
    )
    return jax.shard_map(
        per_device,
        mesh=mesh,
        in_specs=placed,
        out_specs=(P(None, "lon", "lat"), P(None, "lon", "lat"), P(None, "lon", "lat")),
        check_vma=False,
    )
```

```python
import functools

import jax
import jax.numpy as jnp
from jax import lax
from jax.experimental import pallas as pl
from jax.experimental.pallas import tpu as pltpu
from jax.sharding import PartitionSpec as P

BLK = 32
PROBES = 16
HALO = 3
TOP = 8
LANES = 128
EXACT = lax.Precision.HIGHEST
F32 = jnp.float32


def vmem(count):
    return [pl.BlockSpec(memory_space=pltpu.VMEM)] * count


def shape(*dims):
    return jax.ShapeDtypeStruct(dims, F32)


def iota(dims, axis):
    return lax.broadcasted_iota(jnp.int32, dims, axis)


def same_row(ref, row, stride):
    found = []
    for tile in range(ref.shape[0]):
        if stride == 0:
            found.append(ref[tile, pl.ds(row, 8, stride=0), :])
        else:
            found.append(ref[tile, pl.ds(row, 8, stride=stride), :])
    return jnp.concatenate(found, axis=1)


def keep(ref, value):
    for tile in range(ref.shape[0]):
        ref[tile] = value[:, tile * LANES : tile * LANES + LANES]


def row_of(ref, row):
    return jnp.broadcast_to(ref[pl.ds(row, 1), :], (8, ref.shape[1]))


def fetch(sources, targets, sems):
    copies = [
        pltpu.make_async_copy(source, target, sems.at[at])
        for at, (source, target) in enumerate(zip(sources, targets))
    ]
    for copy in copies:
        copy.start()
    for copy in copies:
        copy.wait()


def block_lanes(lat_at, level, width):
    source = iota((width, LANES), 0)
    lane = iota((width, LANES), 1)
    return jnp.where(lane == 64 + 16 * lat_at + 8 * level + source // BLK, 1.0, 0.0).astype(F32)


def block_sums(lat_at, rows):
    total = None
    for level in range(2):
        part = jnp.dot(
            rows[level],
            block_lanes(lat_at, level, rows[level].shape[1]),
            precision=EXACT,
            preferred_element_type=F32,
        )
        total = part if total is None else total + part
    return total


def first_row(row):
    return jnp.where(iota((8, row.shape[1]), 0) == 0, jnp.broadcast_to(row, (8, row.shape[1])), 0.0)


def raw_fields(obs, kap, bits, land):
    return (
        [obs[level] for level in range(2)]
        + [kap[level] for level in range(2)]
        + [bits[word, level].astype(F32) for word in range(2) for level in range(2)]
        + [land[...].astype(F32)]
    )


def prepare_kernel(
    obs_in, kap_in, bits_in, land_in, to_odd, to_even, own, rhs_sums,
    obs, kap, bits, land, ocean, sems,
):
    fetch((obs_in, kap_in, bits_in, land_in), (obs, kap, bits, land), sems)
    lat_at = lax.axis_index("lat")
    even = lax.rem(lax.axis_index("lon"), 2) == 0
    lon_rows, width = land.shape
    fields = raw_fields(obs, kap, bits, land)
    lane = iota((lon_rows, LANES), 1)
    edges = jnp.zeros((lon_rows, LANES), F32)
    for at, field in enumerate(fields):
        first, last = field[:HALO], field[lon_rows - HALO :]
        here = slice(HALO * at, HALO * at + HALO)
        to_odd[here, :] = jnp.where(even, first, last)
        to_even[here, :] = jnp.where(even, last, first)
        low = pltpu.roll(field[:, :LANES], 6 * at, 1) if at else field[:, :LANES]
        high = pltpu.roll(field[:, width - LANES :], (6 * at + 6) % LANES, 1)
        edges = jnp.where((lane >= 6 * at) & (lane < 6 * at + 3), low, edges)
        edges = jnp.where((lane >= 6 * at + 3) & (lane < 6 * at + 6), high, edges)
    to_odd[27:30, :LANES] = jnp.where(even, edges[:HALO], edges[lon_rows - HALO :])
    to_even[27:30, :LANES] = jnp.where(even, edges[lon_rows - HALO :], edges[:HALO])
    keep(ocean, fields[8])
    bit = jnp.left_shift(1, iota((8, width), 0))
    zero = jnp.zeros((8, width), F32)
    sums = {}
    for column in range(2):
        for word in range(2):
            for level in range(2):
                sums[column, word, level] = zero

        def body(row, carry):
            wet = same_row(ocean, row, 0)
            out = []
            for word in range(2):
                for level in range(2):
                    held = row_of(bits.at[word, level], row)
                    out.append(carry[word * 2 + level] + jnp.where((held & bit) != 0, wet, -wet))
            return tuple(out)

        got = lax.fori_loop(column * BLK, column * BLK + BLK, body, (zero,) * 4, unroll=BLK)
        for word in range(2):
            for level in range(2):
                sums[column, word, level] = got[word * 2 + level]
        for level in range(2):
            held = slice(column * BLK, column * BLK + BLK)
            sums[column, 2, level] = first_row(
                jnp.sum(fields[8][held] * fields[level][held], axis=0, keepdims=True)
            )
    rows = [
        jnp.concatenate([sums[column, group, level] for column in range(2) for group in range(3)], axis=0)
        for level in range(2)
    ]
    found = block_sums(lat_at, rows)
    for level in range(2):
        rhs_sums[level] = rows[level]
    own[...] = jnp.zeros(own.shape, F32)
    own[TOP : TOP + lon_rows, :] = edges
    own[24:72, :] = own[24:72, :] + found
    first, last = found[:24], found[24:]
    for target, part in (
        (to_odd, jnp.where(even, first, last)),
        (to_even, jnp.where(even, last, first)),
    ):
        target[32:40, :LANES] = part[:8]
        target[32:40, LANES : 2 * LANES] = part[8:16]
        target[40:48, :LANES] = part[16:24]


def merge_kernel(own, from_odd, from_even, out):
    even = lax.rem(lax.axis_index("lon"), 2) == 0
    odd_part, even_part = from_odd[...], from_even[...]
    prev = jnp.where(even, odd_part, even_part)
    later = jnp.where(even, even_part, odd_part)
    out[...] = own[...]
    for source, row, at in ((prev, TOP - HALO, 0), (later, TOP + 64, 72)):
        out[row : row + HALO, :] = out[row : row + HALO, :] + source[27:30, :LANES]
        out[at : at + 8, :] = out[at : at + 8, :] + source[32:40, :LANES]
        out[at + 8 : at + 16, :] = out[at + 8 : at + 16, :] + source[32:40, LANES : 2 * LANES]
        out[at + 16 : at + 24, :] = out[at + 16 : at + 24, :] + source[40:48, :LANES]


def base_kernel(
    obs_in, kap_in, bits_in, land_in, coarse_in,
    spread, ocean, coef, jacobi, first_rhs, word_bits, begin,
    obs, kap, bits, land, coarse, sems,
):
    fetch(
        (obs_in, kap_in, bits_in, land_in, coarse_in), (obs, kap, bits, land, coarse), sems
    )
    lat_at = lax.axis_index("lat")
    wide = spread.shape[2]
    width = wide - LANES
    per = width // BLK
    lane = iota((32, wide), 1)
    block = jnp.where(lane < width, lane // BLK, -1000)
    block = jnp.where((lane >= width) & (lane < width + HALO), per, block)
    block = jnp.where(lane >= wide - HALO, -1, block)
    chosen = jnp.where(iota((32, wide), 0) == block + per * lat_at, 1.0, 0.0).astype(F32)
    for level in range(2):
        spread[level, 0:64, :] = jnp.zeros((64, wide), F32)
        for other in range(2):
            part = lax.dot_general(
                coarse[level, :, other, :],
                chosen,
                (((0,), (0,)), ((), ())),
                precision=EXACT,
                preferred_element_type=F32,
            )
            for group in range(4):
                at = 64 + 16 * group + 8 * other
                spread[level, at : at + 8, :] = part[8 * group : 8 * group + 8]

    def place(ref, value):
        ends = jnp.zeros((TOP, LANES), value.dtype)
        for tile in range(width // LANES):
            ref[tile, 0:TOP] = ends
            ref[tile, TOP : TOP + land.shape[0]] = value[:, tile * LANES : tile * LANES + LANES]
            ref[tile, TOP + land.shape[0] :] = ends

    wet = land[...].astype(F32)
    place(ocean, wet)
    for level in range(2):
        value = kap[level] + 5.0
        place(coef.at[level], value)
        place(jacobi.at[level], wet / (value * value + 4.0))
        place(first_rhs.at[level], wet * obs[level])
        for word in range(2):
            place(word_bits.at[word, level], bits[word, level])
    bit = jnp.left_shift(1, iota((8, width), 0))

    def body(row, carry):
        for level in range(2):
            weight = same_row(jacobi.at[level], TOP + row, 0)
            for word in range(2):
                held = row_of(bits.at[word, level], row)
                begin[level, word, row] = jnp.where((held & bit) != 0, weight, -weight)
        return carry

    lax.fori_loop(0, land.shape[0], body, 0, unroll=16)


def corrections(gathered, spread, probe_part, even=None):
    total = gathered[0] + gathered[1] + gathered[2] + gathered[3]
    total = jnp.where(iota(total.shape, 1) >= 64, total, 0.0)
    if even is not None:
        first, last = total[:24], total[72:]
        total = jnp.concatenate(
            [jnp.where(even, first, last), total[24:72], jnp.where(even, last, first)], axis=0
        )
    for level in range(2):
        probe_part[level] = jnp.dot(total, spread[level], precision=EXACT, preferred_element_type=F32)


def first_corrections(probe_part, first_part):
    for level in range(2):
        for low, high, at in ((TOP - HALO, TOP, 16), (TOP, 40, 40), (40, 72, 64), (72, 72 + HALO, 88)):
            for tile in range(first_part.shape[1]):
                line = probe_part[level, at : at + 1, tile * LANES : tile * LANES + LANES]
                first_part[level, tile, low:high, :] = jnp.broadcast_to(line, (high - low, LANES))


def stencil(centre, above, below, other, coef, ocean):
    wide = centre.shape[1]
    beside = (above + below) + (pltpu.roll(centre, 1, 1) + pltpu.roll(centre, wide - 1, 1))
    return ocean * (coef * centre - beside - 0.5 * other)


SEGMENTS = ((TOP - HALO, TOP, 0), (TOP, 40, 1), (40, 72, 2), (72, 72 + HALO, 3))


def apply_rows(load, coef, ocean, begin, count, emit):
    for word in range(2):
        held = {}
        for step in range(2):
            for level in range(2):
                held[level, step] = load(level, word, begin - 1 + step)
        for step in range(1, count + 1):
            for level in range(2):
                held[level, step + 1] = load(level, word, begin + step)
            row = begin + step - 1
            sea = same_row(ocean, row, 0)
            for level in range(2):
                emit(
                    level,
                    word,
                    row,
                    stencil(
                        held[level, step],
                        held[level, step - 1],
                        held[level, step + 1],
                        held[1 - level, step],
                        same_row(coef.at[level], row, 0),
                        sea,
                    ),
                )


def image_kernel(
    base_ocean, base_coef, base_jacobi, base_first, base_bits, begin,
    from_odd, from_even, gathered, spread,
    image, first_image, to_odd, to_even, own_sums, row_sums, totals, own_part,
    ocean, coef, jacobi,
    first_rhs, word_bits, direction, inner, first_direction, first_inner, probe_part, first_part,
):
    lat_at = lax.axis_index("lat")
    even = lax.rem(lax.axis_index("lon"), 2) == 0
    lat_count = lax.axis_size("lat")
    tiles, rows, _ = ocean.shape
    width = (tiles - 1) * LANES
    wide = tiles * LANES
    lon_rows = rows - 2 * TOP
    lane = iota((rows, LANES), 1)
    before = gathered[jnp.maximum(lat_at - 1, 0), 0:rows, :]
    after = gathered[jnp.minimum(lat_at + 1, lat_count - 1), 0:rows, :]
    take_before = (lane >= LANES - HALO) & (lat_at > 0)
    take_after = (lane < HALO) & (lat_at < lat_count - 1)
    odd_part, even_part = from_odd[0:32, :], from_even[0:32, :]
    prev = jnp.where(even, odd_part, even_part)
    later = jnp.where(even, even_part, odd_part)

    def outside(at):
        left = pltpu.roll(before, (LANES - HALO - 6 * at - 3) % LANES, 1)
        right = pltpu.roll(after, -6 * at % LANES, 1) if at else after
        tile = jnp.where(take_before, left, jnp.where(take_after, right, 0.0))
        here = slice(HALO * at, HALO * at + HALO)
        return prev[here], later[here], tile

    def fill(ref, base, parts):
        for tile in range(tiles - 1):
            lanes = slice(tile * LANES, tile * LANES + LANES)
            ref[tile] = base[tile]
            ref[tile, TOP - HALO : TOP] = parts[0][:, lanes]
            ref[tile, TOP + lon_rows : TOP + lon_rows + HALO] = parts[1][:, lanes]
        ref[tiles - 1] = parts[2]

    wet = outside(8)
    fill(ocean, base_ocean, wet)
    for level in range(2):
        value = [part + 5.0 for part in outside(2 + level)]
        fill(coef.at[level], base_coef.at[level], value)
        fill(
            jacobi.at[level],
            base_jacobi.at[level],
            [sea / (part * part + 4.0) for sea, part in zip(wet, value)],
        )
        fill(
            first_rhs.at[level],
            base_first.at[level],
            [sea * part for sea, part in zip(wet, outside(level))],
        )
        for word in range(2):
            fill(
                word_bits.at[word, level],
                base_bits.at[word, level],
                [part.astype(jnp.int32) for part in outside(4 + word * 2 + level)],
            )
    corrections(gathered, spread, probe_part)
    first_corrections(probe_part, first_part)
    own_part[...] = probe_part[:, 24:72, :width]
    bit = jnp.left_shift(1, iota((8, wide), 0))
    zero = jnp.zeros((8, width), F32)

    for low, high, column in SEGMENTS:
        own = column in (1, 2)

        def body(row, carry, column=column, own=own):
            sea = same_row(ocean, row, 0)
            for level in range(2):
                weight = same_row(jacobi.at[level], row, 0)
                for word in range(2):
                    if own:
                        place = pl.ds(row, 8, stride=0)
                        part = jacobi[level, tiles - 1, place, :]
                        held = word_bits[word, level, tiles - 1, place, :]
                        part = jnp.where((held & bit[:, :LANES]) != 0, part, -part)
                        fine = jnp.concatenate([begin[level, word, row - TOP], part], axis=1)
                    else:
                        held = same_row(word_bits.at[word, level], row, 0)
                        fine = jnp.where((held & bit) != 0, weight, -weight)
                    at = column * 24 + word * 8
                    direction[level, word, row - (TOP - HALO)] = (
                        fine + sea * probe_part[level, at : at + 8, :]
                    )
            return carry

        lax.fori_loop(low, high, body, 0, unroll=BLK if own else HALO)
    first_gamma = zero
    for step in range(14):
        row = TOP - HALO + step
        sea = same_row(ocean, row, 8)
        for level in range(2):
            rhs = same_row(first_rhs.at[level], row, 8)
            value = same_row(jacobi.at[level], row, 8) * rhs + sea * same_row(first_part.at[level], row, 8)
            first_direction[level, step] = value
            if HALO <= step < HALO + 8:
                first_gamma = first_gamma + (rhs * value)[:, :width]

    def load_direction(level, word, row):
        return direction[level, word, row - (TOP - HALO)]

    def first_body(column, carry, low, count):
        def emit(level, word, row, value):
            inner[level, word, row - (TOP - HALO)] = value

        apply_rows(load_direction, coef, ocean, low + column * count, count, emit)
        return carry

    first_body(0, 0, TOP - 2, 2)
    lax.fori_loop(0, 2, functools.partial(first_body, low=TOP, count=BLK), 0, unroll=2)
    first_body(0, 0, TOP + lon_rows, 2)
    first_norm = zero
    for step in range(1, 13):
        row = TOP - HALO + step
        sea = same_row(ocean, row, 8)
        for level in range(2):
            value = stencil(
                first_direction[level, step],
                first_direction[level, step - 1],
                first_direction[level, step + 1],
                first_direction[1 - level, step],
                same_row(coef.at[level], row, 8),
                sea,
            )
            first_inner[level, step] = value
            if HALO <= step < HALO + 8:
                part = value[:, :width]
                first_norm = first_norm + part * part

    def load_inner(level, word, row):
        return inner[level, word, row - (TOP - HALO)]

    def second_body(column, carry, low, count, own):
        added = {}

        def emit(level, word, row, value):
            image[level, word, row - (TOP - 1)] = value
            if own:
                part = value[:, :width]
                added[level, word] = added[level, word] + part if (level, word) in added else part

        apply_rows(load_inner, coef, ocean, low + column * count, count, emit)
        if own:
            for level in range(2):
                for word in range(2):
                    at = pl.multiple_of(column * 24, 8) + word * 8
                    row_sums[level, pl.ds(at, 8), :] = added[level, word]
        return carry

    second_body(0, 0, TOP - 1, 1, False)
    lax.fori_loop(0, 2, functools.partial(second_body, low=TOP, count=BLK, own=True), 0, unroll=2)
    second_body(0, 0, TOP + lon_rows, 1, False)
    first_sum = [zero, zero]
    for step in range(2, 12):
        row = TOP - HALO + step
        sea = same_row(ocean, row, 8)
        for level in range(2):
            value = stencil(
                first_inner[level, step],
                first_inner[level, step - 1],
                first_inner[level, step + 1],
                first_inner[1 - level, step],
                same_row(coef.at[level], row, 8),
                sea,
            )
            first_image[level, step - 2] = value
            if HALO <= step < HALO + 8:
                first_sum[level] = first_sum[level] + value[:, :width]
    for level in range(2):
        for column in range(2):
            half = first_sum[level][column * 4 : column * 4 + 4]
            row_sums[level, column * 24 + 16 : column * 24 + 24, :] = first_row(
                jnp.sum(half, axis=0, keepdims=True)
            )
    found = block_sums(lat_at, [row_sums[level] for level in range(2)])
    own_sums[...] = found
    to_odd[...] = jnp.where(even, found[:24], found[24:])
    to_even[...] = jnp.where(even, found[24:], found[:24])
    for at, value in enumerate((first_gamma, first_norm)):
        totals[at] = value[:, :LANES] + value[:, LANES:]


BASIS = (0, 256, 272, 288, 304, 312, 344)
PAIRS = [(first, last) for first in range(4) for last in range(first, 4)]
EDGES = (0, 31, 32, 63)


def products_kernel(
    image, first_image, ocean, coef, jacobi, base_first, base_bits, own_part, rhs_sums, row_sums,
    linear, quadratic, edge_value, edge_field, totals, basis,
    field, edge, natural,
):
    tiles, rows, _ = ocean.shape
    width = (tiles - 1) * LANES
    lon_rows = rows - 2 * TOP
    groups = lon_rows // 8
    zero = jnp.zeros((8, width), F32)
    bit = jnp.left_shift(1, iota((8, width), 0))

    def own_rows(ref):
        return jnp.concatenate(
            [ref[tile, TOP : TOP + lon_rows] for tile in range(tiles - 1)], axis=1
        )

    def put(at, value):
        for group in range(groups):
            basis[at + group] = value[8 * group : 8 * group + 8]

    whole = jnp.concatenate([ocean[tile, TOP : TOP + lon_rows] for tile in range(tiles)], axis=1)
    sea = whole[:, :width]
    up = jnp.concatenate([ocean[tile, TOP - 1 : TOP - 1 + lon_rows] for tile in range(tiles - 1)], axis=1)
    down = jnp.concatenate([ocean[tile, TOP + 1 : TOP + 1 + lon_rows] for tile in range(tiles - 1)], axis=1)
    row = iota((lon_rows, width), 0)
    first = lax.rem(row, BLK) == 0
    last = lax.rem(row, BLK) == BLK - 1
    inside = jnp.where(first | last, 0.0, 1.0)
    vertical = jnp.where(first, 0.0, up) + jnp.where(last, 0.0, down)
    across = -sea * (jnp.where(first, up, 0.0) + jnp.where(last, down, 0.0))
    left = -sea * pltpu.roll(whole, 1, 1)[:, :width]
    right = -sea * pltpu.roll(whole, tiles * LANES - 1, 1)[:, :width]
    other = -0.5 * sea
    put(BASIS[4], sea)
    selves = []
    for level in range(2):
        scale = own_rows(coef.at[level])
        put(BASIS[3] + level * groups, 0.5 / (scale * scale + 4.0))
        put(BASIS[1] + level * groups, own_rows(jacobi.at[level]) * own_rows(base_first.at[level]))
        for word in range(2):
            put(
                BASIS[5] + (word * 2 + level) * groups,
                own_rows(base_bits.at[word, level]).astype(F32),
            )
        selves.append(sea * (scale * sea - vertical))
    for at, value in enumerate(selves + [left, right, other]):
        keep(field.at[at], value * inside)
        for place, line in enumerate(EDGES):
            edge_field[place, at : at + 1, :] = value[line : line + 1]
    for place, line in enumerate(EDGES):
        edge_field[place, 5:6, :] = across[line : line + 1]
        edge_field[place, 6:8, :] = jnp.zeros((2, width), F32)
    for level in range(2):
        terms = [selves[level] * inside, left * inside, right * inside, other * inside]
        for at, (one, two) in enumerate(PAIRS):
            product = terms[one] * terms[two]
            for column in range(2):
                quadratic[level, column, at : at + 1, :] = jnp.sum(
                    product[column * BLK : column * BLK + BLK], axis=0, keepdims=True
                )

    def load(level, word, at):
        return same_row(jacobi.at[level], at, 0) * image[level, word, at - (TOP - 1)]

    def body(column, carry):
        carry = list(carry)
        sums = {}

        def emit(level, word, at, value):
            line = at - TOP
            part = value[:, :width]
            carry[2 + word] = carry[2 + word] + part * part
            edge[level, word, line] = part
            for kind, which in enumerate((level, 2, 3, 4)):
                term = part * same_row(field.at[which], line, 0)
                key = level, word, kind
                sums[key] = sums[key] + term if key in sums else term
            source = image[level, word, at - (TOP - 1)][:, :width]
            weighted = same_row(jacobi.at[level], at, 0)[:, :width] * source
            carry[word] = carry[word] + weighted * source
            held = same_row(base_bits.at[word, level], at, 0)
            signed = jnp.where((held & bit) != 0, weighted, -weighted)
            carry[4 + word] = carry[4 + word] + signed
            basis[(level * 2 + word) * lon_rows + line] = signed

        apply_rows(load, coef, ocean, TOP + column * BLK, BLK, emit)
        for (level, word, kind), value in sums.items():
            linear[level, column, word, kind] = value
        return tuple(carry)

    crossed = lax.fori_loop(0, 2, body, (zero,) * 6)
    for place, line in enumerate(EDGES):
        for level in range(2):
            for word in range(2):
                edge_value[place, level, word] = edge[level, word, line]

    first_cross, first_norm = zero, zero
    held = {}
    for level in range(2):
        for step in range(10):
            held[level, step] = same_row(jacobi.at[level], TOP - 1 + step, 8) * first_image[level, step]
    for level in range(2):
        for step in range(8):
            for tile in range(tiles - 1):
                natural[level, tile, pl.ds(step, 8, stride=8), :] = held[level, step + 1][
                    :, tile * LANES : tile * LANES + LANES
                ]
        put(
            BASIS[2] + level * groups,
            jnp.concatenate([natural[level, tile] for tile in range(tiles - 1)], axis=1),
        )
        sums = [zero] * 4
        for step in range(1, 9):
            at = TOP - 1 + step
            value = stencil(
                held[level, step],
                held[level, step - 1],
                held[level, step + 1],
                held[1 - level, step],
                same_row(coef.at[level], at, 8),
                same_row(ocean, at, 8),
            )[:, :width]
            first_norm = first_norm + value * value
            first_cross = first_cross + (held[level, step] * first_image[level, step])[:, :width]
            for kind, which in enumerate((level, 2, 3, 4)):
                sums[kind] = sums[kind] + value * same_row(field.at[which], step - 1, 8)
            if step == 1:
                edge_value[0, level, 2] = first_row(value[0:1])
                edge_value[2, level, 2] = first_row(value[4:5])
            if step == 8:
                edge_value[1, level, 2] = first_row(value[3:4])
                edge_value[3, level, 2] = first_row(value[7:8])
        for kind in range(4):
            for column in range(2):
                half = sums[kind][column * 4 : column * 4 + 4]
                linear[level, column, 2, kind] = first_row(jnp.sum(half, axis=0, keepdims=True))
    weight_sum = sum(
        jnp.sum(own_rows(jacobi.at[level]), axis=0, keepdims=True) for level in range(2)
    )
    gamma, norm = [], []
    for word in range(2):
        gamma.append(jnp.broadcast_to(weight_sum, (8, width)))
        norm.append(crossed[4 + word])
        for level in range(2):
            for column in range(2):
                here = slice(column * 24 + word * 8, column * 24 + word * 8 + 8)
                gamma[word] = gamma[word] + own_part[level, here] * rhs_sums[level, here]
                norm[word] = norm[word] + own_part[level, here] * row_sums[level, here]
    for at, value in enumerate(
        (crossed[0], crossed[1], first_cross, crossed[2], crossed[3], first_norm, *gamma, *norm)
    ):
        totals[at] = value[:, :LANES] + value[:, LANES:]


def norms_kernel(
    gathered, spread, row_sums, linear, quadratic, edge_value, edge_field, early, late,
    packed, own_part, probe_part,
):
    even = lax.rem(lax.axis_index("lon"), 2) == 0
    corrections(gathered, spread, probe_part, even)
    wide = probe_part.shape[2]
    width = wide - LANES
    own_part[...] = probe_part[:, 24:72, :width]
    found = [late[6], late[7], early[0], late[8], late[9], early[1]] + [late[at] for at in range(6)]

    def wide_row(value):
        return jnp.broadcast_to(value, (8, width))

    def own(level, column, group):
        at = column * 24 + group * 8
        return probe_part[level, at : at + 8, :]

    for level in range(2):
        for column in range(2):
            pairs = {
                pair: wide_row(quadratic[level, column, at : at + 1, :]) for at, pair in enumerate(PAIRS)
            }
            for group in range(3):
                here = own(level, column + 1, group)
                terms = [
                    here[:, :width],
                    pltpu.roll(here, 1, 1)[:, :width],
                    pltpu.roll(here, wide - 1, 1)[:, :width],
                    own(1 - level, column + 1, group)[:, :width],
                ]
                at = column * 24 + group * 8
                cross = terms[0] * row_sums[level, at : at + 8, :]
                norm = jnp.zeros((8, width), F32)
                for one in range(4):
                    inside = terms[one] * pairs[one, one]
                    double = linear[level, column, group, one]
                    for two in range(one + 1, 4):
                        double = double + terms[two] * pairs[one, two]
                    norm = norm + terms[one] * (inside + 2.0 * double)
                for place in (2 * column, 2 * column + 1):
                    beyond = (0, 2, 1, 3)[place]
                    value = edge_value[place, level, group]
                    for kind, which in enumerate((level, 2, 3, 4)):
                        value = value + terms[kind] * wide_row(edge_field[place, which : which + 1, :])
                    value = value + own(level, beyond, group)[:, :width] * wide_row(
                        edge_field[place, 5:6, :]
                    )
                    norm = norm + (value * value)
                    mine = edge_value[place, level, group]
                    norm = norm - mine * mine
                found[6 + group] = found[6 + group] + cross[:, :LANES] + cross[:, LANES:]
                found[9 + group] = found[9 + group] + norm[:, :LANES] + norm[:, LANES:]
    lane = iota((8, LANES), 1)
    probe = iota((8, LANES), 0)
    out = jnp.zeros((8, LANES), F32)
    for kind in range(4):
        for group in range(3):
            total = jnp.broadcast_to(
                jnp.sum(found[kind * 3 + group], axis=1, keepdims=True), (8, LANES)
            )
            place = lane == (64 + kind if group == 2 else (kind * 2 + group) * 8 + probe)
            out = out + jnp.where(place, total, 0.0)
    packed[...] = jnp.broadcast_to(jnp.sum(out, axis=0, keepdims=True), packed.shape)


def finish_kernel(packed, early_part, later_part, basis, solution, diagonal, residual, ocean, bits, held, sems):
    _, lon_rows, width = solution.shape
    groups = lon_rows // 8
    total = jnp.broadcast_to(jnp.sum(packed[...], axis=0, keepdims=True), (8, LANES))
    lane = iota((8, LANES), 1)
    probe = iota((8, LANES), 0)

    def get(at):
        return jnp.concatenate([basis[at + group] for group in range(groups)], axis=0)

    def send(which, level):
        target = (solution, diagonal, residual)[which]
        copy = pltpu.make_async_copy(held.at[which, level], target.at[level], sems.at[which, level])
        copy.start()
        return copy

    def weights(group):
        found = []
        for kind in range(4):
            place = lane == (64 + kind if group == 2 else (kind * 2 + group) * 8 + probe)
            found.append(
                jnp.broadcast_to(
                    jnp.sum(jnp.where(place, total, 0.0), axis=1, keepdims=True), (8, LANES)
                )
            )
        gamma, norm, cross, second = found
        ratio = cross / norm
        rest = second - ratio * cross
        alive = rest > 0.0
        later = jnp.where(alive, (norm - ratio * gamma) / jnp.where(alive, rest, 1.0), 0.0)
        earlier = gamma / norm - later * ratio
        return (
            jnp.concatenate([earlier] * (width // LANES), axis=1),
            jnp.concatenate([later] * (width // LANES), axis=1),
        )

    wet = get(BASIS[4])
    keep(ocean, wet)
    for level in range(2):
        for word in range(2):
            bits[word, level] = get(BASIS[5] + (word * 2 + level) * groups).astype(jnp.int32)
    system = [weights(group) for group in range(3)]
    bit = jnp.left_shift(1, iota((8, width), 0))
    row = iota((lon_rows, width), 0)
    share = jnp.sum(system[0][0] + system[1][0], axis=0, keepdims=True)
    share = 2.0 * wet * jnp.broadcast_to(share, (lon_rows, width))
    earlier, later = system[2][0][0:1], system[2][1][0:1]
    copies = []
    for level in range(2):
        lines = [
            earlier * early_part[level, at : at + 1, :] + later * later_part[level, at : at + 1, :]
            for at in (16, 40)
        ]
        held[0, level] = (
            earlier * get(BASIS[1] + level * groups)
            + later * get(BASIS[2] + level * groups)
            + wet * jnp.where(row < BLK, lines[0], lines[1])
        )
        copies.append(send(0, level))
    for level in range(2):
        for column in range(2):
            coarse = []
            for word in range(2):
                at = column * 24 + word * 8
                coarse.append(
                    system[word][0] * early_part[level, at : at + 8, :]
                    + system[word][1] * later_part[level, at : at + 8, :]
                )

            def body(line, carry, coarse=coarse, level=level):
                signs, rest = None, None
                for word in range(2):
                    signed = jnp.where(
                        (row_of(bits.at[word, level], line) & bit) != 0, coarse[word], -coarse[word]
                    )
                    second = system[word][1] * basis[(level * 2 + word) * lon_rows + line]
                    signs = signed if signs is None else signs + signed
                    rest = second if rest is None else rest + second
                whole = same_row(ocean, line, 0) * signs + rest
                held[1, level, pl.ds(line, 1), :] = jnp.sum(whole, axis=0, keepdims=True)
                return carry

            lax.fori_loop(column * BLK, column * BLK + BLK, body, 0, unroll=BLK)
        bound = get(BASIS[3] + level * groups)
        spread = (held[1, level] + share * bound) / PROBES
        held[1, level] = spread
        copies.append(send(1, level))
        held[2, level] = held[0, level] / jnp.maximum(spread, bound)
        copies.append(send(2, level))
    for copy in copies:
        copy.wait()


def call(kernel, outs, scratch=(), outside=0):
    return functools.partial(_run, kernel, outs, scratch, outside)


def _run(kernel, outs, scratch, outside, *args):
    held = [pltpu.with_memory_space_constraint(array, pltpu.HBM) for array in args[:outside]]
    return pl.pallas_call(
        kernel,
        out_shape=outs,
        in_specs=[pl.BlockSpec(memory_space=pltpu.HBM)] * outside + vmem(len(args) - outside),
        out_specs=tuple(vmem(len(outs))),
        scratch_shapes=list(scratch),
        compiler_params=pltpu.CompilerParams(vmem_limit_bytes=24 << 20),
    )(*held, *args[outside:])


def per_device(observed, kappa_squared, probe_bits, land_sea, coarse_block_inverse):
    lon_rows, width = land_sea.shape
    wide = width + LANES
    tiles = wide // LANES
    rows = lon_rows + 2 * TOP
    lon_count = lax.axis_size("lon")
    lat_count = lax.axis_size("lat")
    evens = [(i, i + 1 - 2 * (i % 2)) for i in range(lon_count)]
    odds = [(i, (i - 1 + 2 * (i % 2)) % lon_count) for i in range(lon_count)]
    raw = (observed, kappa_squared, probe_bits, land_sea)
    inside = [pltpu.VMEM(array.shape, array.dtype) for array in raw]
    sems = pltpu.SemaphoreType.DMA((4,))

    to_odd, to_even, own, rhs_sums = call(
        prepare_kernel,
        (shape(48, width), shape(48, width), shape(96, LANES), shape(2, 48, width)),
        [*inside, pltpu.VMEM((width // LANES, lon_rows, LANES), F32), sems],
        4,
    )(*raw)
    from_odd = lax.ppermute(to_odd, "lon", odds)
    from_even = lax.ppermute(to_even, "lon", evens)
    natural = (tiles - 1, rows, LANES)
    spread, *base = call(
        base_kernel,
        (
            shape(2, LANES, wide),
            shape(*natural),
            shape(2, *natural),
            shape(2, *natural),
            shape(2, *natural),
            jax.ShapeDtypeStruct((2, 2, *natural), jnp.int32),
            shape(2, 2, lon_rows, 8, width),
        ),
        [
            *inside,
            pltpu.VMEM(coarse_block_inverse.shape, F32),
            pltpu.SemaphoreType.DMA((5,)),
        ],
        5,
    )(*raw, coarse_block_inverse)
    (merged,) = call(merge_kernel, (shape(96, LANES),))(own, from_odd, from_even)
    gathered = lax.all_gather(merged, "lat")
    probe_parts = pltpu.VMEM((2, 96, wide), F32)
    first_parts = pltpu.VMEM((2, tiles, rows, LANES), F32)
    image, first_image, to_odd, to_even, own_sums, row_sums, early, own_part, ocean, coef, jacobi = call(
        image_kernel,
        (
            shape(2, 2, lon_rows + 2, 8, wide),
            shape(2, 10, 8, wide),
            shape(24, LANES),
            shape(24, LANES),
            shape(48, LANES),
            shape(2, 48, width),
            shape(2, 8, LANES),
            shape(2, 48, width),
            shape(tiles, rows, LANES),
            shape(2, tiles, rows, LANES),
            shape(2, tiles, rows, LANES),
        ),
        [
            first_parts,
            pltpu.VMEM((2, 2, tiles, rows, LANES), jnp.int32),
            pltpu.VMEM((2, 2, lon_rows + 2 * HALO, 8, wide), F32),
            pltpu.VMEM((2, 2, lon_rows + 2 * HALO, 8, wide), F32),
            pltpu.VMEM((2, 14, 8, wide), F32),
            pltpu.VMEM((2, 14, 8, wide), F32),
            probe_parts,
            first_parts,
        ],
    )(*base, from_odd, from_even, gathered, spread)

    sums_odd = lax.ppermute(to_odd, "lon", odds)
    sums_even = lax.ppermute(to_even, "lon", evens)
    blocks = width // LANES
    linear, quadratic, edge_value, edge_field, late, basis = call(
        products_kernel,
        (
            shape(2, 2, 3, 4, 8, width),
            shape(2, 2, 16, width),
            shape(4, 2, 3, 8, width),
            shape(4, 8, width),
            shape(10, 8, LANES),
            shape(BASIS[-1], 8, width),
        ),
        [
            pltpu.VMEM((5, blocks, lon_rows, LANES), F32),
            pltpu.VMEM((2, 2, lon_rows, 8, width), F32),
            pltpu.VMEM((2, blocks, lon_rows, LANES), F32),
        ],
    )(image, first_image, ocean, coef, jacobi, base[3], base[4], own_part, rhs_sums, row_sums)
    sums = lax.all_gather(jnp.concatenate([sums_odd, own_sums, sums_even], axis=0), "lat")
    packed, later_part = call(
        norms_kernel, (shape(lon_count * lat_count, LANES), shape(2, 48, width)), [probe_parts]
    )(
        sums, spread, row_sums, linear, quadratic, edge_value, edge_field, early, late
    )
    everyone = lax.all_to_all(packed, ("lon", "lat"), 0, 0)
    return tuple(
        pl.pallas_call(
            finish_kernel,
            out_shape=(shape(2, lon_rows, width),) * 3,
            in_specs=vmem(4),
            out_specs=tuple([pl.BlockSpec(memory_space=pltpu.HBM)] * 3),
            scratch_shapes=[
                pltpu.VMEM((blocks, lon_rows, LANES), F32),
                pltpu.VMEM((2, 2, lon_rows, width), jnp.int32),
                pltpu.VMEM((3, 2, lon_rows, width), F32),
                pltpu.SemaphoreType.DMA((3, 2)),
            ],
            compiler_params=pltpu.CompilerParams(vmem_limit_bytes=24 << 20),
        )(everyone, own_part, later_part, basis)
    )


def solution(mesh):
    placed = (
        P(None, "lon", "lat"),
        P(None, "lon", "lat"),
        P(None, None, "lon", "lat"),
        P("lon", "lat"),
        P(),
    )
    return jax.shard_map(
        per_device,
        mesh=mesh,
        in_specs=placed,
        out_specs=(P(None, "lon", "lat"), P(None, "lon", "lat"), P(None, "lon", "lat")),
        check_vma=False,
    )
```

```python
import functools

import jax
import jax.numpy as jnp
from jax import lax
from jax.experimental import pallas as pl
from jax.experimental.pallas import tpu as pltpu
from jax.sharding import PartitionSpec as P

BLK = 32
PROBES = 16
HALO = 3
TOP = 8
LANES = 128
EXACT = lax.Precision.HIGHEST
F32 = jnp.float32


def vmem(count):
    return [pl.BlockSpec(memory_space=pltpu.VMEM)] * count


def shape(*dims):
    return jax.ShapeDtypeStruct(dims, F32)


def iota(dims, axis):
    return lax.broadcasted_iota(jnp.int32, dims, axis)


def same_row(ref, row, stride):
    found = []
    for tile in range(ref.shape[0]):
        if stride == 0:
            found.append(ref[tile, pl.ds(row, 8, stride=0), :])
        else:
            found.append(ref[tile, pl.ds(row, 8, stride=stride), :])
    return jnp.concatenate(found, axis=1)


def keep(ref, value):
    for tile in range(ref.shape[0]):
        ref[tile] = value[:, tile * LANES : tile * LANES + LANES]


def row_of(ref, row):
    return jnp.broadcast_to(ref[pl.ds(row, 1), :], (8, ref.shape[1]))


def fetch(sources, targets, sems):
    copies = [
        pltpu.make_async_copy(source, target, sems.at[at])
        for at, (source, target) in enumerate(zip(sources, targets))
    ]
    for copy in copies:
        copy.start()
    for copy in copies:
        copy.wait()


def block_lanes(lat_at, level, width):
    source = iota((width, LANES), 0)
    lane = iota((width, LANES), 1)
    return jnp.where(lane == 64 + 16 * lat_at + 8 * level + source // BLK, 1.0, 0.0).astype(F32)


def block_sums(lat_at, rows):
    total = None
    for level in range(2):
        part = jnp.dot(
            rows[level],
            block_lanes(lat_at, level, rows[level].shape[1]),
            precision=EXACT,
            preferred_element_type=F32,
        )
        total = part if total is None else total + part
    return total


def first_row(row):
    return jnp.where(iota((8, row.shape[1]), 0) == 0, jnp.broadcast_to(row, (8, row.shape[1])), 0.0)


def raw_fields(obs, kap, bits, land):
    return (
        [obs[level] for level in range(2)]
        + [kap[level] for level in range(2)]
        + [bits[word, level].astype(F32) for word in range(2) for level in range(2)]
        + [land[...].astype(F32)]
    )


def prepare_kernel(
    obs_in, kap_in, bits_in, land_in, to_odd, to_even, own, rhs_sums,
    obs, kap, bits, land, ocean, sems,
):
    copies = [
        pltpu.make_async_copy(source, target, sems.at[at])
        for at, (source, target) in enumerate(
            ((land_in, land), (bits_in, bits), (obs_in, obs), (kap_in, kap))
        )
    ]
    for copy in copies:
        copy.start()
    lat_at = lax.axis_index("lat")
    even = lax.rem(lax.axis_index("lon"), 2) == 0
    lon_rows, width = land.shape
    copies[0].wait()
    copies[1].wait()
    keep(ocean, land[...].astype(F32))
    bit = jnp.left_shift(1, iota((8, width), 0))
    zero = jnp.zeros((8, width), F32)
    sums = {}
    for column in range(2):

        def body(row, carry):
            wet = same_row(ocean, row, 0)
            out = []
            for word in range(2):
                for level in range(2):
                    held = row_of(bits.at[word, level], row)
                    out.append(carry[word * 2 + level] + jnp.where((held & bit) != 0, wet, -wet))
            return tuple(out)

        got = lax.fori_loop(column * BLK, column * BLK + BLK, body, (zero,) * 4, unroll=BLK)
        for word in range(2):
            for level in range(2):
                sums[column, word, level] = got[word * 2 + level]
    copies[2].wait()
    copies[3].wait()
    fields = raw_fields(obs, kap, bits, land)
    lane = iota((lon_rows, LANES), 1)
    edges = jnp.zeros((lon_rows, LANES), F32)
    for at, field in enumerate(fields):
        first, last = field[:HALO], field[lon_rows - HALO :]
        here = slice(HALO * at, HALO * at + HALO)
        to_odd[here, :] = jnp.where(even, first, last)
        to_even[here, :] = jnp.where(even, last, first)
        low = pltpu.roll(field[:, :LANES], 6 * at, 1) if at else field[:, :LANES]
        high = pltpu.roll(field[:, width - LANES :], (6 * at + 6) % LANES, 1)
        edges = jnp.where((lane >= 6 * at) & (lane < 6 * at + 3), low, edges)
        edges = jnp.where((lane >= 6 * at + 3) & (lane < 6 * at + 6), high, edges)
    to_odd[27:30, :LANES] = jnp.where(even, edges[:HALO], edges[lon_rows - HALO :])
    to_even[27:30, :LANES] = jnp.where(even, edges[lon_rows - HALO :], edges[:HALO])
    for column in range(2):
        for level in range(2):
            held = slice(column * BLK, column * BLK + BLK)
            sums[column, 2, level] = first_row(
                jnp.sum(fields[8][held] * fields[level][held], axis=0, keepdims=True)
            )
    rows = [
        jnp.concatenate([sums[column, group, level] for column in range(2) for group in range(3)], axis=0)
        for level in range(2)
    ]
    found = block_sums(lat_at, rows)
    for level in range(2):
        rhs_sums[level] = rows[level]
    own[...] = jnp.zeros(own.shape, F32)
    own[TOP : TOP + lon_rows, :] = edges
    own[24:72, :] = own[24:72, :] + found
    first, last = found[:24], found[24:]
    for target, part in (
        (to_odd, jnp.where(even, first, last)),
        (to_even, jnp.where(even, last, first)),
    ):
        target[32:40, :LANES] = part[:8]
        target[32:40, LANES : 2 * LANES] = part[8:16]
        target[40:48, :LANES] = part[16:24]


def merge_kernel(own, from_odd, from_even, out):
    even = lax.rem(lax.axis_index("lon"), 2) == 0
    odd_part, even_part = from_odd[...], from_even[...]
    prev = jnp.where(even, odd_part, even_part)
    later = jnp.where(even, even_part, odd_part)
    out[...] = own[...]
    for source, row, at in ((prev, TOP - HALO, 0), (later, TOP + 64, 72)):
        out[row : row + HALO, :] = out[row : row + HALO, :] + source[27:30, :LANES]
        out[at : at + 8, :] = out[at : at + 8, :] + source[32:40, :LANES]
        out[at + 8 : at + 16, :] = out[at + 8 : at + 16, :] + source[32:40, LANES : 2 * LANES]
        out[at + 16 : at + 24, :] = out[at + 16 : at + 24, :] + source[40:48, :LANES]


def base_kernel(
    obs_in, kap_in, bits_in, land_in, coarse_in,
    spread, ocean, coef, jacobi, first_rhs, word_bits, begin,
    obs, kap, bits, land, coarse, sems,
):
    fetch(
        (obs_in, kap_in, bits_in, land_in, coarse_in), (obs, kap, bits, land, coarse), sems
    )
    lat_at = lax.axis_index("lat")
    wide = spread.shape[2]
    width = wide - LANES
    per = width // BLK
    lane = iota((32, wide), 1)
    block = jnp.where(lane < width, lane // BLK, -1000)
    block = jnp.where((lane >= width) & (lane < width + HALO), per, block)
    block = jnp.where(lane >= wide - HALO, -1, block)
    chosen = jnp.where(iota((32, wide), 0) == block + per * lat_at, 1.0, 0.0).astype(F32)
    for level in range(2):
        spread[level, 0:64, :] = jnp.zeros((64, wide), F32)
        for other in range(2):
            part = lax.dot_general(
                coarse[level, :, other, :],
                chosen,
                (((0,), (0,)), ((), ())),
                precision=EXACT,
                preferred_element_type=F32,
            )
            for group in range(4):
                at = 64 + 16 * group + 8 * other
                spread[level, at : at + 8, :] = part[8 * group : 8 * group + 8]

    def place(ref, value):
        ends = jnp.zeros((TOP, LANES), value.dtype)
        for tile in range(width // LANES):
            ref[tile, 0:TOP] = ends
            ref[tile, TOP : TOP + land.shape[0]] = value[:, tile * LANES : tile * LANES + LANES]
            ref[tile, TOP + land.shape[0] :] = ends

    wet = land[...].astype(F32)
    place(ocean, wet)
    for level in range(2):
        value = kap[level] + 5.0
        place(coef.at[level], value)
        place(jacobi.at[level], wet / (value * value + 4.0))
        place(first_rhs.at[level], wet * obs[level])
        for word in range(2):
            place(word_bits.at[word, level], bits[word, level])
    bit = jnp.left_shift(1, iota((8, width), 0))

    def body(row, carry):
        for level in range(2):
            weight = same_row(jacobi.at[level], TOP + row, 0)
            for word in range(2):
                held = row_of(bits.at[word, level], row)
                begin[level, word, row] = jnp.where((held & bit) != 0, weight, -weight)
        return carry

    lax.fori_loop(0, land.shape[0], body, 0, unroll=16)


def corrections(gathered, spread, probe_part, even=None):
    total = gathered[0] + gathered[1] + gathered[2] + gathered[3]
    high = iota(total.shape, 1) >= 64
    received = jnp.where(high, total, 0.0)
    if even is None:
        total = received
    else:
        own = jnp.where(high, pltpu.roll(total, 64, 1), 0.0)
        first, last = received[:24], received[24:]
        total = jnp.concatenate(
            [jnp.where(even, first, last), own, jnp.where(even, last, first)], axis=0
        )
    for level in range(2):
        probe_part[level] = jnp.dot(total, spread[level], precision=EXACT, preferred_element_type=F32)


def first_corrections(probe_part, first_part):
    for level in range(2):
        for low, high, at in ((TOP - HALO, TOP, 16), (TOP, 40, 40), (40, 72, 64), (72, 72 + HALO, 88)):
            for tile in range(first_part.shape[1]):
                line = probe_part[level, at : at + 1, tile * LANES : tile * LANES + LANES]
                first_part[level, tile, low:high, :] = jnp.broadcast_to(line, (high - low, LANES))


def stencil(centre, above, below, other, coef, ocean):
    wide = centre.shape[1]
    beside = (above + below) + (pltpu.roll(centre, 1, 1) + pltpu.roll(centre, wide - 1, 1))
    return ocean * (coef * centre - beside - 0.5 * other)


SEGMENTS = ((TOP - HALO, TOP, 0), (TOP, 40, 1), (40, 72, 2), (72, 72 + HALO, 3))


def apply_rows(load, coef, ocean, begin, count, emit):
    for word in range(2):
        held = {}
        for step in range(2):
            for level in range(2):
                held[level, step] = load(level, word, begin - 1 + step)
        for step in range(1, count + 1):
            for level in range(2):
                held[level, step + 1] = load(level, word, begin + step)
            row = begin + step - 1
            sea = same_row(ocean, row, 0)
            for level in range(2):
                emit(
                    level,
                    word,
                    row,
                    stencil(
                        held[level, step],
                        held[level, step - 1],
                        held[level, step + 1],
                        held[1 - level, step],
                        same_row(coef.at[level], row, 0),
                        sea,
                    ),
                )


def image_kernel(
    base_ocean, base_coef, base_jacobi, base_first, base_bits, begin,
    from_odd, from_even, gathered, spread,
    image, first_image, to_odd, to_even, own_sums, row_sums, totals, own_part,
    ocean, coef, jacobi,
    first_rhs, word_bits, direction, inner, first_direction, first_inner, probe_part, first_part,
):
    lat_at = lax.axis_index("lat")
    even = lax.rem(lax.axis_index("lon"), 2) == 0
    lat_count = lax.axis_size("lat")
    tiles, rows, _ = ocean.shape
    width = (tiles - 1) * LANES
    wide = tiles * LANES
    lon_rows = rows - 2 * TOP
    lane = iota((rows, LANES), 1)
    before = gathered[jnp.maximum(lat_at - 1, 0), 0:rows, :]
    after = gathered[jnp.minimum(lat_at + 1, lat_count - 1), 0:rows, :]
    take_before = (lane >= LANES - HALO) & (lat_at > 0)
    take_after = (lane < HALO) & (lat_at < lat_count - 1)
    odd_part, even_part = from_odd[0:32, :], from_even[0:32, :]
    prev = jnp.where(even, odd_part, even_part)
    later = jnp.where(even, even_part, odd_part)

    def outside(at):
        left = pltpu.roll(before, (LANES - HALO - 6 * at - 3) % LANES, 1)
        right = pltpu.roll(after, -6 * at % LANES, 1) if at else after
        tile = jnp.where(take_before, left, jnp.where(take_after, right, 0.0))
        here = slice(HALO * at, HALO * at + HALO)
        return prev[here], later[here], tile

    def fill(ref, base, parts):
        for tile in range(tiles - 1):
            lanes = slice(tile * LANES, tile * LANES + LANES)
            ref[tile] = base[tile]
            ref[tile, TOP - HALO : TOP] = parts[0][:, lanes]
            ref[tile, TOP + lon_rows : TOP + lon_rows + HALO] = parts[1][:, lanes]
        ref[tiles - 1] = parts[2]

    wet = outside(8)
    fill(ocean, base_ocean, wet)
    for level in range(2):
        value = [part + 5.0 for part in outside(2 + level)]
        fill(coef.at[level], base_coef.at[level], value)
        fill(
            jacobi.at[level],
            base_jacobi.at[level],
            [sea / (part * part + 4.0) for sea, part in zip(wet, value)],
        )
        fill(
            first_rhs.at[level],
            base_first.at[level],
            [sea * part for sea, part in zip(wet, outside(level))],
        )
        for word in range(2):
            fill(
                word_bits.at[word, level],
                base_bits.at[word, level],
                [part.astype(jnp.int32) for part in outside(4 + word * 2 + level)],
            )
    corrections(gathered, spread, probe_part)
    first_corrections(probe_part, first_part)
    own_part[...] = probe_part[:, 24:72, :width]
    bit = jnp.left_shift(1, iota((8, wide), 0))
    zero = jnp.zeros((8, width), F32)

    for low, high, column in SEGMENTS:
        own = column in (1, 2)

        def body(row, carry, column=column, own=own):
            sea = same_row(ocean, row, 0)
            for level in range(2):
                weight = same_row(jacobi.at[level], row, 0)
                for word in range(2):
                    if own:
                        place = pl.ds(row, 8, stride=0)
                        part = jacobi[level, tiles - 1, place, :]
                        held = word_bits[word, level, tiles - 1, place, :]
                        part = jnp.where((held & bit[:, :LANES]) != 0, part, -part)
                        fine = jnp.concatenate([begin[level, word, row - TOP], part], axis=1)
                    else:
                        held = same_row(word_bits.at[word, level], row, 0)
                        fine = jnp.where((held & bit) != 0, weight, -weight)
                    at = column * 24 + word * 8
                    direction[level, word, row - (TOP - HALO)] = (
                        fine + sea * probe_part[level, at : at + 8, :]
                    )
            return carry

        lax.fori_loop(low, high, body, 0, unroll=BLK if own else HALO)
    first_gamma = zero
    for step in range(14):
        row = TOP - HALO + step
        sea = same_row(ocean, row, 8)
        for level in range(2):
            rhs = same_row(first_rhs.at[level], row, 8)
            value = same_row(jacobi.at[level], row, 8) * rhs + sea * same_row(first_part.at[level], row, 8)
            first_direction[level, step] = value
            if HALO <= step < HALO + 8:
                first_gamma = first_gamma + (rhs * value)[:, :width]

    def load_direction(level, word, row):
        return direction[level, word, row - (TOP - HALO)]

    def first_body(column, carry, low, count):
        def emit(level, word, row, value):
            inner[level, word, row - (TOP - HALO)] = value

        apply_rows(load_direction, coef, ocean, low + column * count, count, emit)
        return carry

    first_body(0, 0, TOP - 2, 2)
    lax.fori_loop(0, 2, functools.partial(first_body, low=TOP, count=BLK), 0, unroll=2)
    first_body(0, 0, TOP + lon_rows, 2)
    first_norm = zero
    for step in range(1, 13):
        row = TOP - HALO + step
        sea = same_row(ocean, row, 8)
        for level in range(2):
            value = stencil(
                first_direction[level, step],
                first_direction[level, step - 1],
                first_direction[level, step + 1],
                first_direction[1 - level, step],
                same_row(coef.at[level], row, 8),
                sea,
            )
            first_inner[level, step] = value
            if HALO <= step < HALO + 8:
                part = value[:, :width]
                first_norm = first_norm + part * part

    def load_inner(level, word, row):
        return inner[level, word, row - (TOP - HALO)]

    def second_body(column, carry, low, count, own):
        added = {}

        def emit(level, word, row, value):
            image[level, word, row - (TOP - 1)] = value
            if own:
                part = value[:, :width]
                added[level, word] = added[level, word] + part if (level, word) in added else part

        apply_rows(load_inner, coef, ocean, low + column * count, count, emit)
        if own:
            for level in range(2):
                for word in range(2):
                    at = pl.multiple_of(column * 24, 8) + word * 8
                    row_sums[level, pl.ds(at, 8), :] = added[level, word]
        return carry

    second_body(0, 0, TOP - 1, 1, False)
    lax.fori_loop(0, 2, functools.partial(second_body, low=TOP, count=BLK, own=True), 0, unroll=2)
    second_body(0, 0, TOP + lon_rows, 1, False)
    first_sum = [zero, zero]
    for step in range(2, 12):
        row = TOP - HALO + step
        sea = same_row(ocean, row, 8)
        for level in range(2):
            value = stencil(
                first_inner[level, step],
                first_inner[level, step - 1],
                first_inner[level, step + 1],
                first_inner[1 - level, step],
                same_row(coef.at[level], row, 8),
                sea,
            )
            first_image[level, step - 2] = value
            if HALO <= step < HALO + 8:
                first_sum[level] = first_sum[level] + value[:, :width]
    for level in range(2):
        for column in range(2):
            half = first_sum[level][column * 4 : column * 4 + 4]
            row_sums[level, column * 24 + 16 : column * 24 + 24, :] = first_row(
                jnp.sum(half, axis=0, keepdims=True)
            )
    found = block_sums(lat_at, [row_sums[level] for level in range(2)])
    own_sums[...] = pltpu.roll(found, 64, 1)
    to_odd[...] = jnp.where(even, found[:24], found[24:])
    to_even[...] = jnp.where(even, found[24:], found[:24])
    for at, value in enumerate((first_gamma, first_norm)):
        totals[at] = value[:, :LANES] + value[:, LANES:]


BASIS = (0, 256, 272, 288, 304, 312, 344)
PAIRS = [(first, last) for first in range(4) for last in range(first, 4)]
EDGES = (0, 31, 32, 63)


def products_kernel(
    image, first_image, ocean, coef, jacobi, base_first, base_bits, own_part, rhs_sums, row_sums,
    linear, quadratic, edge_value, edge_field, totals, basis,
    field, edge, natural,
):
    tiles, rows, _ = ocean.shape
    width = (tiles - 1) * LANES
    lon_rows = rows - 2 * TOP
    groups = lon_rows // 8
    zero = jnp.zeros((8, width), F32)
    bit = jnp.left_shift(1, iota((8, width), 0))

    def own_rows(ref):
        return jnp.concatenate(
            [ref[tile, TOP : TOP + lon_rows] for tile in range(tiles - 1)], axis=1
        )

    def put(at, value):
        for group in range(groups):
            basis[at + group] = value[8 * group : 8 * group + 8]

    whole = jnp.concatenate([ocean[tile, TOP : TOP + lon_rows] for tile in range(tiles)], axis=1)
    sea = whole[:, :width]
    up = jnp.concatenate([ocean[tile, TOP - 1 : TOP - 1 + lon_rows] for tile in range(tiles - 1)], axis=1)
    down = jnp.concatenate([ocean[tile, TOP + 1 : TOP + 1 + lon_rows] for tile in range(tiles - 1)], axis=1)
    row = iota((lon_rows, width), 0)
    first = lax.rem(row, BLK) == 0
    last = lax.rem(row, BLK) == BLK - 1
    inside = jnp.where(first | last, 0.0, 1.0)
    vertical = jnp.where(first, 0.0, up) + jnp.where(last, 0.0, down)
    across = -sea * (jnp.where(first, up, 0.0) + jnp.where(last, down, 0.0))
    left = -sea * pltpu.roll(whole, 1, 1)[:, :width]
    right = -sea * pltpu.roll(whole, tiles * LANES - 1, 1)[:, :width]
    other = -0.5 * sea
    put(BASIS[4], sea)
    selves = []
    for level in range(2):
        scale = own_rows(coef.at[level])
        put(BASIS[3] + level * groups, 0.5 / (scale * scale + 4.0))
        put(BASIS[1] + level * groups, own_rows(jacobi.at[level]) * own_rows(base_first.at[level]))
        for word in range(2):
            put(
                BASIS[5] + (word * 2 + level) * groups,
                own_rows(base_bits.at[word, level]).astype(F32),
            )
        selves.append(sea * (scale * sea - vertical))
    for at, value in enumerate(selves + [left, right, other]):
        keep(field.at[at], value * inside)
        for place, line in enumerate(EDGES):
            edge_field[place, at : at + 1, :] = value[line : line + 1]
    for place, line in enumerate(EDGES):
        edge_field[place, 5:6, :] = across[line : line + 1]
        edge_field[place, 6:8, :] = jnp.zeros((2, width), F32)
    for level in range(2):
        terms = [selves[level] * inside, left * inside, right * inside, other * inside]
        for at, (one, two) in enumerate(PAIRS):
            product = terms[one] * terms[two]
            for column in range(2):
                quadratic[level, column, at : at + 1, :] = jnp.sum(
                    product[column * BLK : column * BLK + BLK], axis=0, keepdims=True
                )

    def load(level, word, at):
        return same_row(jacobi.at[level], at, 0) * image[level, word, at - (TOP - 1)]

    def body(column, carry):
        carry = list(carry)
        sums = {}

        def emit(level, word, at, value):
            line = at - TOP
            part = value[:, :width]
            carry[2 + word] = carry[2 + word] + part * part
            edge[level, word, line] = part
            for kind, which in enumerate((level, 2, 3, 4)):
                term = part * same_row(field.at[which], line, 0)
                key = level, word, kind
                sums[key] = sums[key] + term if key in sums else term
            source = image[level, word, at - (TOP - 1)][:, :width]
            weighted = same_row(jacobi.at[level], at, 0)[:, :width] * source
            carry[word] = carry[word] + weighted * source
            held = same_row(base_bits.at[word, level], at, 0)
            signed = jnp.where((held & bit) != 0, weighted, -weighted)
            carry[4 + word] = carry[4 + word] + signed
            basis[(level * 2 + word) * lon_rows + line] = signed

        apply_rows(load, coef, ocean, TOP + column * BLK, BLK, emit)
        for (level, word, kind), value in sums.items():
            linear[level, column, word, kind] = value
        return tuple(carry)

    crossed = lax.fori_loop(0, 2, body, (zero,) * 6)
    for place, line in enumerate(EDGES):
        for level in range(2):
            for word in range(2):
                edge_value[place, level, word] = edge[level, word, line]

    first_cross, first_norm = zero, zero
    held = {}
    for level in range(2):
        for step in range(10):
            held[level, step] = same_row(jacobi.at[level], TOP - 1 + step, 8) * first_image[level, step]
    for level in range(2):
        for step in range(8):
            for tile in range(tiles - 1):
                natural[level, tile, pl.ds(step, 8, stride=8), :] = held[level, step + 1][
                    :, tile * LANES : tile * LANES + LANES
                ]
        put(
            BASIS[2] + level * groups,
            jnp.concatenate([natural[level, tile] for tile in range(tiles - 1)], axis=1),
        )
        sums = [zero] * 4
        for step in range(1, 9):
            at = TOP - 1 + step
            value = stencil(
                held[level, step],
                held[level, step - 1],
                held[level, step + 1],
                held[1 - level, step],
                same_row(coef.at[level], at, 8),
                same_row(ocean, at, 8),
            )[:, :width]
            first_norm = first_norm + value * value
            first_cross = first_cross + (held[level, step] * first_image[level, step])[:, :width]
            for kind, which in enumerate((level, 2, 3, 4)):
                sums[kind] = sums[kind] + value * same_row(field.at[which], step - 1, 8)
            if step == 1:
                edge_value[0, level, 2] = first_row(value[0:1])
                edge_value[2, level, 2] = first_row(value[4:5])
            if step == 8:
                edge_value[1, level, 2] = first_row(value[3:4])
                edge_value[3, level, 2] = first_row(value[7:8])
        for kind in range(4):
            for column in range(2):
                half = sums[kind][column * 4 : column * 4 + 4]
                linear[level, column, 2, kind] = first_row(jnp.sum(half, axis=0, keepdims=True))
    weight_sum = sum(
        jnp.sum(own_rows(jacobi.at[level]), axis=0, keepdims=True) for level in range(2)
    )
    gamma, norm = [], []
    for word in range(2):
        gamma.append(jnp.broadcast_to(weight_sum, (8, width)))
        norm.append(crossed[4 + word])
        for level in range(2):
            for column in range(2):
                here = slice(column * 24 + word * 8, column * 24 + word * 8 + 8)
                gamma[word] = gamma[word] + own_part[level, here] * rhs_sums[level, here]
                norm[word] = norm[word] + own_part[level, here] * row_sums[level, here]
    for at, value in enumerate(
        (crossed[0], crossed[1], first_cross, crossed[2], crossed[3], first_norm, *gamma, *norm)
    ):
        totals[at] = value[:, :LANES] + value[:, LANES:]


def norms_kernel(
    gathered, spread, row_sums, linear, quadratic, edge_value, edge_field, early, late,
    packed, own_part, probe_part,
):
    even = lax.rem(lax.axis_index("lon"), 2) == 0
    corrections(gathered, spread, probe_part, even)
    wide = probe_part.shape[2]
    width = wide - LANES
    own_part[...] = probe_part[:, 24:72, :width]
    found = [late[6], late[7], early[0], late[8], late[9], early[1]] + [late[at] for at in range(6)]

    def wide_row(value):
        return jnp.broadcast_to(value, (8, width))

    def own(level, column, group):
        at = column * 24 + group * 8
        return probe_part[level, at : at + 8, :]

    for level in range(2):
        for column in range(2):
            pairs = {
                pair: wide_row(quadratic[level, column, at : at + 1, :]) for at, pair in enumerate(PAIRS)
            }
            for group in range(3):
                here = own(level, column + 1, group)
                terms = [
                    here[:, :width],
                    pltpu.roll(here, 1, 1)[:, :width],
                    pltpu.roll(here, wide - 1, 1)[:, :width],
                    own(1 - level, column + 1, group)[:, :width],
                ]
                at = column * 24 + group * 8
                cross = terms[0] * row_sums[level, at : at + 8, :]
                norm = jnp.zeros((8, width), F32)
                for one in range(4):
                    inside = terms[one] * pairs[one, one]
                    double = linear[level, column, group, one]
                    for two in range(one + 1, 4):
                        double = double + terms[two] * pairs[one, two]
                    norm = norm + terms[one] * (inside + 2.0 * double)
                for place in (2 * column, 2 * column + 1):
                    beyond = (0, 2, 1, 3)[place]
                    value = edge_value[place, level, group]
                    for kind, which in enumerate((level, 2, 3, 4)):
                        value = value + terms[kind] * wide_row(edge_field[place, which : which + 1, :])
                    value = value + own(level, beyond, group)[:, :width] * wide_row(
                        edge_field[place, 5:6, :]
                    )
                    norm = norm + (value * value)
                    mine = edge_value[place, level, group]
                    norm = norm - mine * mine
                found[6 + group] = found[6 + group] + cross[:, :LANES] + cross[:, LANES:]
                found[9 + group] = found[9 + group] + norm[:, :LANES] + norm[:, LANES:]
    lane = iota((8, LANES), 1)
    probe = iota((8, LANES), 0)
    out = jnp.zeros((8, LANES), F32)
    for kind in range(4):
        for group in range(3):
            total = jnp.broadcast_to(
                jnp.sum(found[kind * 3 + group], axis=1, keepdims=True), (8, LANES)
            )
            place = lane == (64 + kind if group == 2 else (kind * 2 + group) * 8 + probe)
            out = out + jnp.where(place, total, 0.0)
    packed[...] = jnp.broadcast_to(jnp.sum(out, axis=0, keepdims=True), packed.shape)


def finish_kernel(packed, early_part, later_part, basis, solution, diagonal, residual, ocean, bits, held, sems):
    _, lon_rows, width = solution.shape
    groups = lon_rows // 8
    total = jnp.broadcast_to(jnp.sum(packed[...], axis=0, keepdims=True), (8, LANES))
    lane = iota((8, LANES), 1)
    probe = iota((8, LANES), 0)

    def get(at):
        return jnp.concatenate([basis[at + group] for group in range(groups)], axis=0)

    def send(which, level):
        target = (solution, diagonal, residual)[which]
        copy = pltpu.make_async_copy(held.at[which, level], target.at[level], sems.at[which, level])
        copy.start()
        return copy

    def weights(group):
        found = []
        for kind in range(4):
            place = lane == (64 + kind if group == 2 else (kind * 2 + group) * 8 + probe)
            found.append(
                jnp.broadcast_to(
                    jnp.sum(jnp.where(place, total, 0.0), axis=1, keepdims=True), (8, LANES)
                )
            )
        gamma, norm, cross, second = found
        ratio = cross / norm
        rest = second - ratio * cross
        alive = rest > 0.0
        later = jnp.where(alive, (norm - ratio * gamma) / jnp.where(alive, rest, 1.0), 0.0)
        earlier = gamma / norm - later * ratio
        return (
            jnp.concatenate([earlier] * (width // LANES), axis=1),
            jnp.concatenate([later] * (width // LANES), axis=1),
        )

    wet = get(BASIS[4])
    keep(ocean, wet)
    for level in range(2):
        for word in range(2):
            bits[word, level] = get(BASIS[5] + (word * 2 + level) * groups).astype(jnp.int32)
    system = [weights(group) for group in range(3)]
    bit = jnp.left_shift(1, iota((8, width), 0))
    row = iota((lon_rows, width), 0)
    share = jnp.sum(system[0][0] + system[1][0], axis=0, keepdims=True)
    share = 2.0 * wet * jnp.broadcast_to(share, (lon_rows, width))
    earlier, later = system[2][0][0:1], system[2][1][0:1]
    copies = []
    for level in range(2):
        lines = [
            earlier * early_part[level, at : at + 1, :] + later * later_part[level, at : at + 1, :]
            for at in (16, 40)
        ]
        held[0, level] = (
            earlier * get(BASIS[1] + level * groups)
            + later * get(BASIS[2] + level * groups)
            + wet * jnp.where(row < BLK, lines[0], lines[1])
        )
        copies.append(send(0, level))
    for level in range(2):
        for column in range(2):
            coarse = []
            for word in range(2):
                at = column * 24 + word * 8
                coarse.append(
                    system[word][0] * early_part[level, at : at + 8, :]
                    + system[word][1] * later_part[level, at : at + 8, :]
                )

            def body(line, carry, coarse=coarse, level=level):
                signs, rest = None, None
                for word in range(2):
                    signed = jnp.where(
                        (row_of(bits.at[word, level], line) & bit) != 0, coarse[word], -coarse[word]
                    )
                    second = system[word][1] * basis[(level * 2 + word) * lon_rows + line]
                    signs = signed if signs is None else signs + signed
                    rest = second if rest is None else rest + second
                whole = same_row(ocean, line, 0) * signs + rest
                held[1, level, pl.ds(line, 1), :] = jnp.sum(whole, axis=0, keepdims=True)
                return carry

            lax.fori_loop(column * BLK, column * BLK + BLK, body, 0, unroll=BLK)
        bound = get(BASIS[3] + level * groups)
        spread = (held[1, level] + share * bound) / PROBES
        held[1, level] = spread
        copies.append(send(1, level))
        held[2, level] = held[0, level] / jnp.maximum(spread, bound)
        copies.append(send(2, level))
    for copy in copies:
        copy.wait()


def call(kernel, outs, scratch=(), outside=0):
    return functools.partial(_run, kernel, outs, scratch, outside)


def _run(kernel, outs, scratch, outside, *args):
    held = [pltpu.with_memory_space_constraint(array, pltpu.HBM) for array in args[:outside]]
    return pl.pallas_call(
        kernel,
        out_shape=outs,
        in_specs=[pl.BlockSpec(memory_space=pltpu.HBM)] * outside + vmem(len(args) - outside),
        out_specs=tuple(vmem(len(outs))),
        scratch_shapes=list(scratch),
        compiler_params=pltpu.CompilerParams(vmem_limit_bytes=24 << 20),
    )(*held, *args[outside:])


def per_device(observed, kappa_squared, probe_bits, land_sea, coarse_block_inverse):
    lon_rows, width = land_sea.shape
    wide = width + LANES
    tiles = wide // LANES
    rows = lon_rows + 2 * TOP
    lon_count = lax.axis_size("lon")
    lat_count = lax.axis_size("lat")
    evens = [(i, i + 1 - 2 * (i % 2)) for i in range(lon_count)]
    odds = [(i, (i - 1 + 2 * (i % 2)) % lon_count) for i in range(lon_count)]
    raw = (observed, kappa_squared, probe_bits, land_sea)
    inside = [pltpu.VMEM(array.shape, array.dtype) for array in raw]
    sems = pltpu.SemaphoreType.DMA((4,))

    to_odd, to_even, own, rhs_sums = call(
        prepare_kernel,
        (shape(48, width), shape(48, width), shape(96, LANES), shape(2, 48, width)),
        [*inside, pltpu.VMEM((width // LANES, lon_rows, LANES), F32), sems],
        4,
    )(*raw)
    from_odd = lax.ppermute(to_odd, "lon", odds)
    from_even = lax.ppermute(to_even, "lon", evens)
    natural = (tiles - 1, rows, LANES)
    spread, *base = call(
        base_kernel,
        (
            shape(2, LANES, wide),
            shape(*natural),
            shape(2, *natural),
            shape(2, *natural),
            shape(2, *natural),
            jax.ShapeDtypeStruct((2, 2, *natural), jnp.int32),
            shape(2, 2, lon_rows, 8, width),
        ),
        [
            *inside,
            pltpu.VMEM(coarse_block_inverse.shape, F32),
            pltpu.SemaphoreType.DMA((5,)),
        ],
        5,
    )(*raw, coarse_block_inverse)
    (merged,) = call(merge_kernel, (shape(96, LANES),))(own, from_odd, from_even)
    gathered = lax.all_gather(merged, "lat")
    probe_parts = pltpu.VMEM((2, 96, wide), F32)
    first_parts = pltpu.VMEM((2, tiles, rows, LANES), F32)
    image, first_image, to_odd, to_even, own_sums, row_sums, early, own_part, ocean, coef, jacobi = call(
        image_kernel,
        (
            shape(2, 2, lon_rows + 2, 8, wide),
            shape(2, 10, 8, wide),
            shape(24, LANES),
            shape(24, LANES),
            shape(48, LANES),
            shape(2, 48, width),
            shape(2, 8, LANES),
            shape(2, 48, width),
            shape(tiles, rows, LANES),
            shape(2, tiles, rows, LANES),
            shape(2, tiles, rows, LANES),
        ),
        [
            first_parts,
            pltpu.VMEM((2, 2, tiles, rows, LANES), jnp.int32),
            pltpu.VMEM((2, 2, lon_rows + 2 * HALO, 8, wide), F32),
            pltpu.VMEM((2, 2, lon_rows + 2 * HALO, 8, wide), F32),
            pltpu.VMEM((2, 14, 8, wide), F32),
            pltpu.VMEM((2, 14, 8, wide), F32),
            probe_parts,
            first_parts,
        ],
    )(*base, from_odd, from_even, gathered, spread)

    sums_odd = lax.ppermute(to_odd, "lon", odds)
    sums_even = lax.ppermute(to_even, "lon", evens)
    blocks = width // LANES
    linear, quadratic, edge_value, edge_field, late, basis = call(
        products_kernel,
        (
            shape(2, 2, 3, 4, 8, width),
            shape(2, 2, 16, width),
            shape(4, 2, 3, 8, width),
            shape(4, 8, width),
            shape(10, 8, LANES),
            shape(BASIS[-1], 8, width),
        ),
        [
            pltpu.VMEM((5, blocks, lon_rows, LANES), F32),
            pltpu.VMEM((2, 2, lon_rows, 8, width), F32),
            pltpu.VMEM((2, blocks, lon_rows, LANES), F32),
        ],
    )(image, first_image, ocean, coef, jacobi, base[3], base[4], own_part, rhs_sums, row_sums)
    sums = lax.all_gather(jnp.concatenate([sums_odd + own_sums[:24], sums_even + own_sums[24:]], axis=0), "lat")
    packed, later_part = call(
        norms_kernel, (shape(lon_count * lat_count, LANES), shape(2, 48, width)), [probe_parts]
    )(
        sums, spread, row_sums, linear, quadratic, edge_value, edge_field, early, late
    )
    everyone = lax.all_to_all(packed, ("lon", "lat"), 0, 0)
    return tuple(
        pl.pallas_call(
            finish_kernel,
            out_shape=(shape(2, lon_rows, width),) * 3,
            in_specs=vmem(4),
            out_specs=tuple([pl.BlockSpec(memory_space=pltpu.HBM)] * 3),
            scratch_shapes=[
                pltpu.VMEM((blocks, lon_rows, LANES), F32),
                pltpu.VMEM((2, 2, lon_rows, width), jnp.int32),
                pltpu.VMEM((3, 2, lon_rows, width), F32),
                pltpu.SemaphoreType.DMA((3, 2)),
            ],
            compiler_params=pltpu.CompilerParams(vmem_limit_bytes=24 << 20),
        )(everyone, own_part, later_part, basis)
    )


def solution(mesh):
    placed = (
        P(None, "lon", "lat"),
        P(None, "lon", "lat"),
        P(None, None, "lon", "lat"),
        P("lon", "lat"),
        P(),
    )
    return jax.shard_map(
        per_device,
        mesh=mesh,
        in_specs=placed,
        out_specs=(P(None, "lon", "lat"), P(None, "lon", "lat"), P(None, "lon", "lat")),
        check_vma=False,
    )
```

```python
import functools

import jax
import jax.numpy as jnp
from jax import lax
from jax.experimental import pallas as pl
from jax.experimental.pallas import tpu as pltpu
from jax.sharding import PartitionSpec as P

BLK = 32
PROBES = 16
HALO = 3
TOP = 8
LANES = 128
EXACT = lax.Precision.HIGHEST
F32 = jnp.float32


def vmem(count):
    return [pl.BlockSpec(memory_space=pltpu.VMEM)] * count


def shape(*dims):
    return jax.ShapeDtypeStruct(dims, F32)


def iota(dims, axis):
    return lax.broadcasted_iota(jnp.int32, dims, axis)


def same_row(ref, row, stride):
    found = []
    for tile in range(ref.shape[0]):
        if stride == 0:
            found.append(jnp.broadcast_to(ref[tile, pl.ds(row, 1), :], (8, LANES)))
        else:
            found.append(ref[tile, pl.ds(row, 8, stride=stride), :])
    return jnp.concatenate(found, axis=1)


def keep(ref, value):
    for tile in range(ref.shape[0]):
        ref[tile] = value[:, tile * LANES : tile * LANES + LANES]


def row_of(ref, row):
    return jnp.broadcast_to(ref[pl.ds(row, 1), :], (8, ref.shape[1]))


def fetch(sources, targets, sems):
    copies = [
        pltpu.make_async_copy(source, target, sems.at[at])
        for at, (source, target) in enumerate(zip(sources, targets))
    ]
    for copy in copies:
        copy.start()
    for copy in copies:
        copy.wait()


def block_lanes(lat_at, level, width):
    source = iota((width, LANES), 0)
    lane = iota((width, LANES), 1)
    return jnp.where(lane == 64 + 16 * lat_at + 8 * level + source // BLK, 1.0, 0.0).astype(F32)


def block_sums(lat_at, rows):
    total = None
    for level in range(2):
        part = jnp.dot(
            rows[level],
            block_lanes(lat_at, level, rows[level].shape[1]),
            precision=EXACT,
            preferred_element_type=F32,
        )
        total = part if total is None else total + part
    return total


def first_row(row):
    return jnp.where(iota((8, row.shape[1]), 0) == 0, jnp.broadcast_to(row, (8, row.shape[1])), 0.0)


def raw_fields(obs, kap, bits, land):
    return (
        [obs[level] for level in range(2)]
        + [kap[level] for level in range(2)]
        + [bits[word, level].astype(F32) for word in range(2) for level in range(2)]
        + [land[...].astype(F32)]
    )


def prepare_kernel(
    obs_in, kap_in, bits_in, land_in, to_odd, to_even, own, rhs_sums,
    obs, kap, bits, land, ocean, sems,
):
    copies = [
        pltpu.make_async_copy(source, target, sems.at[at])
        for at, (source, target) in enumerate(
            ((land_in, land), (bits_in, bits), (obs_in, obs), (kap_in, kap))
        )
    ]
    for copy in copies:
        copy.start()
    lat_at = lax.axis_index("lat")
    even = lax.rem(lax.axis_index("lon"), 2) == 0
    lon_rows, width = land.shape
    copies[0].wait()
    copies[1].wait()
    keep(ocean, land[...].astype(F32))
    bit = jnp.left_shift(1, iota((8, width), 0))
    zero = jnp.zeros((8, width), F32)
    sums = {}
    for column in range(2):

        def body(row, carry):
            wet = same_row(ocean, row, 0)
            out = []
            for word in range(2):
                for level in range(2):
                    held = row_of(bits.at[word, level], row)
                    out.append(carry[word * 2 + level] + jnp.where((held & bit) != 0, wet, -wet))
            return tuple(out)

        got = lax.fori_loop(column * BLK, column * BLK + BLK, body, (zero,) * 4, unroll=BLK)
        for word in range(2):
            for level in range(2):
                sums[column, word, level] = got[word * 2 + level]
    copies[2].wait()
    copies[3].wait()
    fields = raw_fields(obs, kap, bits, land)
    lane = iota((lon_rows, LANES), 1)
    edges = jnp.zeros((lon_rows, LANES), F32)
    for at, field in enumerate(fields):
        first, last = field[:HALO], field[lon_rows - HALO :]
        here = slice(HALO * at, HALO * at + HALO)
        to_odd[here, :] = jnp.where(even, first, last)
        to_even[here, :] = jnp.where(even, last, first)
        low = pltpu.roll(field[:, :LANES], 6 * at, 1) if at else field[:, :LANES]
        high = pltpu.roll(field[:, width - LANES :], (6 * at + 6) % LANES, 1)
        edges = jnp.where((lane >= 6 * at) & (lane < 6 * at + 3), low, edges)
        edges = jnp.where((lane >= 6 * at + 3) & (lane < 6 * at + 6), high, edges)
    to_odd[27:30, :LANES] = jnp.where(even, edges[:HALO], edges[lon_rows - HALO :])
    to_even[27:30, :LANES] = jnp.where(even, edges[lon_rows - HALO :], edges[:HALO])
    for column in range(2):
        for level in range(2):
            held = slice(column * BLK, column * BLK + BLK)
            sums[column, 2, level] = first_row(
                jnp.sum(fields[8][held] * fields[level][held], axis=0, keepdims=True)
            )
    rows = [
        jnp.concatenate([sums[column, group, level] for column in range(2) for group in range(3)], axis=0)
        for level in range(2)
    ]
    found = block_sums(lat_at, rows)
    for level in range(2):
        rhs_sums[level] = rows[level]
    own[...] = jnp.zeros(own.shape, F32)
    own[TOP : TOP + lon_rows, :] = edges
    own[24:72, :] = own[24:72, :] + found
    first, last = found[:24], found[24:]
    for target, part in (
        (to_odd, jnp.where(even, first, last)),
        (to_even, jnp.where(even, last, first)),
    ):
        target[32:40, :LANES] = part[:8]
        target[32:40, LANES : 2 * LANES] = part[8:16]
        target[40:48, :LANES] = part[16:24]


def merge_kernel(own, from_odd, from_even, out):
    even = lax.rem(lax.axis_index("lon"), 2) == 0
    odd_part, even_part = from_odd[...], from_even[...]
    prev = jnp.where(even, odd_part, even_part)
    later = jnp.where(even, even_part, odd_part)
    out[...] = own[...]
    for source, row, at in ((prev, TOP - HALO, 0), (later, TOP + 64, 72)):
        out[row : row + HALO, :] = out[row : row + HALO, :] + source[27:30, :LANES]
        out[at : at + 8, :] = out[at : at + 8, :] + source[32:40, :LANES]
        out[at + 8 : at + 16, :] = out[at + 8 : at + 16, :] + source[32:40, LANES : 2 * LANES]
        out[at + 16 : at + 24, :] = out[at + 16 : at + 24, :] + source[40:48, :LANES]


def base_kernel(
    obs_in, kap_in, bits_in, land_in, coarse_in,
    spread, ocean, coef, jacobi, first_rhs, word_bits, begin,
    obs, kap, bits, land, coarse, sems,
):
    fetch(
        (obs_in, kap_in, bits_in, land_in, coarse_in), (obs, kap, bits, land, coarse), sems
    )
    lat_at = lax.axis_index("lat")
    wide = spread.shape[2]
    width = wide - LANES
    per = width // BLK
    lane = iota((32, wide), 1)
    block = jnp.where(lane < width, lane // BLK, -1000)
    block = jnp.where((lane >= width) & (lane < width + HALO), per, block)
    block = jnp.where(lane >= wide - HALO, -1, block)
    chosen = jnp.where(iota((32, wide), 0) == block + per * lat_at, 1.0, 0.0).astype(F32)
    for level in range(2):
        spread[level, 0:64, :] = jnp.zeros((64, wide), F32)
        for other in range(2):
            part = lax.dot_general(
                coarse[level, :, other, :],
                chosen,
                (((0,), (0,)), ((), ())),
                precision=EXACT,
                preferred_element_type=F32,
            )
            for group in range(4):
                at = 64 + 16 * group + 8 * other
                spread[level, at : at + 8, :] = part[8 * group : 8 * group + 8]

    def place(ref, value):
        ends = jnp.zeros((TOP, LANES), value.dtype)
        for tile in range(width // LANES):
            ref[tile, 0:TOP] = ends
            ref[tile, TOP : TOP + land.shape[0]] = value[:, tile * LANES : tile * LANES + LANES]
            ref[tile, TOP + land.shape[0] :] = ends

    wet = land[...].astype(F32)
    place(ocean, wet)
    for level in range(2):
        value = kap[level] + 5.0
        place(coef.at[level], value)
        place(jacobi.at[level], wet / (value * value + 4.0))
        place(first_rhs.at[level], wet * obs[level])
        for word in range(2):
            place(word_bits.at[word, level], bits[word, level])
    bit = jnp.left_shift(1, iota((8, width), 0))

    def body(row, carry):
        for level in range(2):
            weight = same_row(jacobi.at[level], TOP + row, 0)
            for word in range(2):
                held = row_of(bits.at[word, level], row)
                begin[level, word, row] = jnp.where((held & bit) != 0, weight, -weight)
        return carry

    lax.fori_loop(0, land.shape[0], body, 0, unroll=16)


def corrections(gathered, spread, probe_part, even=None):
    total = gathered[0] + gathered[1] + gathered[2] + gathered[3]
    high = iota(total.shape, 1) >= 64
    received = jnp.where(high, total, 0.0)
    if even is None:
        total = received
    else:
        own = jnp.where(high, pltpu.roll(total, 64, 1), 0.0)
        first, last = received[:24], received[24:]
        total = jnp.concatenate(
            [jnp.where(even, first, last), own, jnp.where(even, last, first)], axis=0
        )
    for level in range(2):
        probe_part[level] = jnp.dot(total, spread[level], precision=EXACT, preferred_element_type=F32)


def first_corrections(probe_part, first_part):
    for level in range(2):
        for low, high, at in ((TOP - HALO, TOP, 16), (TOP, 40, 40), (40, 72, 64), (72, 72 + HALO, 88)):
            for tile in range(first_part.shape[1]):
                line = probe_part[level, at : at + 1, tile * LANES : tile * LANES + LANES]
                first_part[level, tile, low:high, :] = jnp.broadcast_to(line, (high - low, LANES))


def stencil(centre, above, below, other, coef, ocean):
    wide = centre.shape[1]
    beside = (above + below) + (pltpu.roll(centre, 1, 1) + pltpu.roll(centre, wide - 1, 1))
    return ocean * (coef * centre - beside - 0.5 * other)


SEGMENTS = ((TOP - HALO, TOP, 0), (TOP, 40, 1), (40, 72, 2), (72, 72 + HALO, 3))


def apply_rows(load, coef, ocean, begin, count, emit):
    for word in range(2):
        held = {}
        for step in range(2):
            for level in range(2):
                held[level, step] = load(level, word, begin - 1 + step)
        for step in range(1, count + 1):
            for level in range(2):
                held[level, step + 1] = load(level, word, begin + step)
            row = begin + step - 1
            sea = same_row(ocean, row, 0)
            for level in range(2):
                emit(
                    level,
                    word,
                    row,
                    stencil(
                        held[level, step],
                        held[level, step - 1],
                        held[level, step + 1],
                        held[1 - level, step],
                        same_row(coef.at[level], row, 0),
                        sea,
                    ),
                )


def image_kernel(
    base_ocean, base_coef, base_jacobi, base_first, base_bits, begin,
    from_odd, from_even, gathered, spread,
    image, first_image, to_odd, to_even, own_sums, row_sums, totals, own_part,
    ocean, coef, jacobi,
    first_rhs, word_bits, direction, inner, first_direction, first_inner, probe_part, first_part,
):
    lat_at = lax.axis_index("lat")
    even = lax.rem(lax.axis_index("lon"), 2) == 0
    lat_count = lax.axis_size("lat")
    tiles, rows, _ = ocean.shape
    width = (tiles - 1) * LANES
    wide = tiles * LANES
    lon_rows = rows - 2 * TOP
    lane = iota((rows, LANES), 1)
    before = gathered[jnp.maximum(lat_at - 1, 0), 0:rows, :]
    after = gathered[jnp.minimum(lat_at + 1, lat_count - 1), 0:rows, :]
    take_before = (lane >= LANES - HALO) & (lat_at > 0)
    take_after = (lane < HALO) & (lat_at < lat_count - 1)
    odd_part, even_part = from_odd[0:32, :], from_even[0:32, :]
    prev = jnp.where(even, odd_part, even_part)
    later = jnp.where(even, even_part, odd_part)

    def outside(at):
        left = pltpu.roll(before, (LANES - HALO - 6 * at - 3) % LANES, 1)
        right = pltpu.roll(after, -6 * at % LANES, 1) if at else after
        tile = jnp.where(take_before, left, jnp.where(take_after, right, 0.0))
        here = slice(HALO * at, HALO * at + HALO)
        return prev[here], later[here], tile

    def fill(ref, base, parts):
        for tile in range(tiles - 1):
            lanes = slice(tile * LANES, tile * LANES + LANES)
            ref[tile] = base[tile]
            ref[tile, TOP - HALO : TOP] = parts[0][:, lanes]
            ref[tile, TOP + lon_rows : TOP + lon_rows + HALO] = parts[1][:, lanes]
        ref[tiles - 1] = parts[2]

    wet = outside(8)
    fill(ocean, base_ocean, wet)
    for level in range(2):
        value = [part + 5.0 for part in outside(2 + level)]
        fill(coef.at[level], base_coef.at[level], value)
        fill(
            jacobi.at[level],
            base_jacobi.at[level],
            [sea / (part * part + 4.0) for sea, part in zip(wet, value)],
        )
        fill(
            first_rhs.at[level],
            base_first.at[level],
            [sea * part for sea, part in zip(wet, outside(level))],
        )
        for word in range(2):
            fill(
                word_bits.at[word, level],
                base_bits.at[word, level],
                [part.astype(jnp.int32) for part in outside(4 + word * 2 + level)],
            )
    corrections(gathered, spread, probe_part)
    first_corrections(probe_part, first_part)
    own_part[...] = probe_part[:, 24:72, :width]
    bit = jnp.left_shift(1, iota((8, wide), 0))
    zero = jnp.zeros((8, width), F32)

    for low, high, column in SEGMENTS:
        own = column in (1, 2)

        def body(row, carry, column=column, own=own):
            sea = same_row(ocean, row, 0)
            for level in range(2):
                weight = same_row(jacobi.at[level], row, 0)
                for word in range(2):
                    if own:
                        part = row_of(jacobi.at[level, tiles - 1], row)
                        held = row_of(word_bits.at[word, level, tiles - 1], row)
                        part = jnp.where((held & bit[:, :LANES]) != 0, part, -part)
                        fine = jnp.concatenate([begin[level, word, row - TOP], part], axis=1)
                    else:
                        held = same_row(word_bits.at[word, level], row, 0)
                        fine = jnp.where((held & bit) != 0, weight, -weight)
                    at = column * 24 + word * 8
                    direction[level, word, row - (TOP - HALO)] = (
                        fine + sea * probe_part[level, at : at + 8, :]
                    )
            return carry

        lax.fori_loop(low, high, body, 0, unroll=BLK if own else HALO)
    first_gamma = zero
    for step in range(14):
        row = TOP - HALO + step
        sea = same_row(ocean, row, 8)
        for level in range(2):
            rhs = same_row(first_rhs.at[level], row, 8)
            value = same_row(jacobi.at[level], row, 8) * rhs + sea * same_row(first_part.at[level], row, 8)
            first_direction[level, step] = value
            if HALO <= step < HALO + 8:
                first_gamma = first_gamma + (rhs * value)[:, :width]

    def load_direction(level, word, row):
        return direction[level, word, row - (TOP - HALO)]

    def first_body(column, carry, low, count):
        def emit(level, word, row, value):
            inner[level, word, row - (TOP - HALO)] = value

        apply_rows(load_direction, coef, ocean, low + column * count, count, emit)
        return carry

    first_body(0, 0, TOP - 2, 2)
    lax.fori_loop(0, 2, functools.partial(first_body, low=TOP, count=BLK), 0, unroll=2)
    first_body(0, 0, TOP + lon_rows, 2)
    first_norm = zero
    for step in range(1, 13):
        row = TOP - HALO + step
        sea = same_row(ocean, row, 8)
        for level in range(2):
            value = stencil(
                first_direction[level, step],
                first_direction[level, step - 1],
                first_direction[level, step + 1],
                first_direction[1 - level, step],
                same_row(coef.at[level], row, 8),
                sea,
            )
            first_inner[level, step] = value
            if HALO <= step < HALO + 8:
                part = value[:, :width]
                first_norm = first_norm + part * part

    def load_inner(level, word, row):
        return inner[level, word, row - (TOP - HALO)]

    def second_body(column, carry, low, count, own):
        added = {}

        def emit(level, word, row, value):
            image[level, word, row - (TOP - 1)] = value
            if own:
                part = value[:, :width]
                added[level, word] = added[level, word] + part if (level, word) in added else part

        apply_rows(load_inner, coef, ocean, low + column * count, count, emit)
        if own:
            for level in range(2):
                for word in range(2):
                    at = pl.multiple_of(column * 24, 8) + word * 8
                    row_sums[level, pl.ds(at, 8), :] = added[level, word]
        return carry

    second_body(0, 0, TOP - 1, 1, False)
    lax.fori_loop(0, 2, functools.partial(second_body, low=TOP, count=BLK, own=True), 0, unroll=2)
    second_body(0, 0, TOP + lon_rows, 1, False)
    first_sum = [zero, zero]
    for step in range(2, 12):
        row = TOP - HALO + step
        sea = same_row(ocean, row, 8)
        for level in range(2):
            value = stencil(
                first_inner[level, step],
                first_inner[level, step - 1],
                first_inner[level, step + 1],
                first_inner[1 - level, step],
                same_row(coef.at[level], row, 8),
                sea,
            )
            first_image[level, step - 2] = value
            if HALO <= step < HALO + 8:
                first_sum[level] = first_sum[level] + value[:, :width]
    for level in range(2):
        for column in range(2):
            half = first_sum[level][column * 4 : column * 4 + 4]
            row_sums[level, column * 24 + 16 : column * 24 + 24, :] = first_row(
                jnp.sum(half, axis=0, keepdims=True)
            )
    found = block_sums(lat_at, [row_sums[level] for level in range(2)])
    own_sums[...] = pltpu.roll(found, 64, 1)
    to_odd[...] = jnp.where(even, found[:24], found[24:])
    to_even[...] = jnp.where(even, found[24:], found[:24])
    for at, value in enumerate((first_gamma, first_norm)):
        totals[at] = value[:, :LANES] + value[:, LANES:]


BASIS = (0, 256, 272, 288, 304, 312, 344)
PAIRS = [(first, last) for first in range(4) for last in range(first, 4)]
EDGES = (0, 31, 32, 63)


def products_kernel(
    image, first_image, ocean, coef, jacobi, base_first, base_bits, own_part, rhs_sums, row_sums,
    linear, quadratic, edge_value, edge_field, totals, basis,
    field, edge, natural,
):
    tiles, rows, _ = ocean.shape
    width = (tiles - 1) * LANES
    lon_rows = rows - 2 * TOP
    groups = lon_rows // 8
    zero = jnp.zeros((8, width), F32)
    bit = jnp.left_shift(1, iota((8, width), 0))

    def own_rows(ref):
        return jnp.concatenate(
            [ref[tile, TOP : TOP + lon_rows] for tile in range(tiles - 1)], axis=1
        )

    def put(at, value):
        for group in range(groups):
            basis[at + group] = value[8 * group : 8 * group + 8]

    whole = jnp.concatenate([ocean[tile, TOP : TOP + lon_rows] for tile in range(tiles)], axis=1)
    sea = whole[:, :width]
    up = jnp.concatenate([ocean[tile, TOP - 1 : TOP - 1 + lon_rows] for tile in range(tiles - 1)], axis=1)
    down = jnp.concatenate([ocean[tile, TOP + 1 : TOP + 1 + lon_rows] for tile in range(tiles - 1)], axis=1)
    row = iota((lon_rows, width), 0)
    first = lax.rem(row, BLK) == 0
    last = lax.rem(row, BLK) == BLK - 1
    inside = jnp.where(first | last, 0.0, 1.0)
    vertical = jnp.where(first, 0.0, up) + jnp.where(last, 0.0, down)
    across = -sea * (jnp.where(first, up, 0.0) + jnp.where(last, down, 0.0))
    left = -sea * pltpu.roll(whole, 1, 1)[:, :width]
    right = -sea * pltpu.roll(whole, tiles * LANES - 1, 1)[:, :width]
    other = -0.5 * sea
    put(BASIS[4], sea)
    selves = []
    for level in range(2):
        scale = own_rows(coef.at[level])
        put(BASIS[3] + level * groups, 0.5 / (scale * scale + 4.0))
        put(BASIS[1] + level * groups, own_rows(jacobi.at[level]) * own_rows(base_first.at[level]))
        for word in range(2):
            put(
                BASIS[5] + (word * 2 + level) * groups,
                own_rows(base_bits.at[word, level]).astype(F32),
            )
        selves.append(sea * (scale * sea - vertical))
    for at, value in enumerate(selves + [left, right, other]):
        keep(field.at[at], value * inside)
        for place, line in enumerate(EDGES):
            edge_field[place, at : at + 1, :] = value[line : line + 1]
    for place, line in enumerate(EDGES):
        edge_field[place, 5:6, :] = across[line : line + 1]
        edge_field[place, 6:8, :] = jnp.zeros((2, width), F32)
    for level in range(2):
        terms = [selves[level] * inside, left * inside, right * inside, other * inside]
        for at, (one, two) in enumerate(PAIRS):
            product = terms[one] * terms[two]
            for column in range(2):
                quadratic[level, column, at : at + 1, :] = jnp.sum(
                    product[column * BLK : column * BLK + BLK], axis=0, keepdims=True
                )

    def load(level, word, at):
        return same_row(jacobi.at[level], at, 0) * image[level, word, at - (TOP - 1)]

    def body(column, carry):
        carry = list(carry)
        sums = {}

        def emit(level, word, at, value):
            line = at - TOP
            part = value[:, :width]
            carry[2 + word] = carry[2 + word] + part * part
            edge[level, word, line] = part
            for kind, which in enumerate((level, 2, 3, 4)):
                term = part * same_row(field.at[which], line, 0)
                key = level, word, kind
                sums[key] = sums[key] + term if key in sums else term
            source = image[level, word, at - (TOP - 1)][:, :width]
            weighted = same_row(jacobi.at[level], at, 0)[:, :width] * source
            carry[word] = carry[word] + weighted * source
            held = same_row(base_bits.at[word, level], at, 0)
            signed = jnp.where((held & bit) != 0, weighted, -weighted)
            carry[4 + word] = carry[4 + word] + signed
            basis[(level * 2 + word) * lon_rows + line] = signed

        apply_rows(load, coef, ocean, TOP + column * BLK, BLK, emit)
        for (level, word, kind), value in sums.items():
            linear[level, column, word, kind] = value
        return tuple(carry)

    crossed = lax.fori_loop(0, 2, body, (zero,) * 6)
    for place, line in enumerate(EDGES):
        for level in range(2):
            for word in range(2):
                edge_value[place, level, word] = edge[level, word, line]

    first_cross, first_norm = zero, zero
    held = {}
    for level in range(2):
        for step in range(10):
            held[level, step] = same_row(jacobi.at[level], TOP - 1 + step, 8) * first_image[level, step]
    for level in range(2):
        for step in range(8):
            for tile in range(tiles - 1):
                natural[level, tile, pl.ds(step, 8, stride=8), :] = held[level, step + 1][
                    :, tile * LANES : tile * LANES + LANES
                ]
        put(
            BASIS[2] + level * groups,
            jnp.concatenate([natural[level, tile] for tile in range(tiles - 1)], axis=1),
        )
        sums = [zero] * 4
        for step in range(1, 9):
            at = TOP - 1 + step
            value = stencil(
                held[level, step],
                held[level, step - 1],
                held[level, step + 1],
                held[1 - level, step],
                same_row(coef.at[level], at, 8),
                same_row(ocean, at, 8),
            )[:, :width]
            first_norm = first_norm + value * value
            first_cross = first_cross + (held[level, step] * first_image[level, step])[:, :width]
            for kind, which in enumerate((level, 2, 3, 4)):
                sums[kind] = sums[kind] + value * same_row(field.at[which], step - 1, 8)
            if step == 1:
                edge_value[0, level, 2] = first_row(value[0:1])
                edge_value[2, level, 2] = first_row(value[4:5])
            if step == 8:
                edge_value[1, level, 2] = first_row(value[3:4])
                edge_value[3, level, 2] = first_row(value[7:8])
        for kind in range(4):
            for column in range(2):
                half = sums[kind][column * 4 : column * 4 + 4]
                linear[level, column, 2, kind] = first_row(jnp.sum(half, axis=0, keepdims=True))
    weight_sum = sum(
        jnp.sum(own_rows(jacobi.at[level]), axis=0, keepdims=True) for level in range(2)
    )
    gamma, norm = [], []
    for word in range(2):
        gamma.append(jnp.broadcast_to(weight_sum, (8, width)))
        norm.append(crossed[4 + word])
        for level in range(2):
            for column in range(2):
                here = slice(column * 24 + word * 8, column * 24 + word * 8 + 8)
                gamma[word] = gamma[word] + own_part[level, here] * rhs_sums[level, here]
                norm[word] = norm[word] + own_part[level, here] * row_sums[level, here]
    for at, value in enumerate(
        (crossed[0], crossed[1], first_cross, crossed[2], crossed[3], first_norm, *gamma, *norm)
    ):
        totals[at] = value[:, :LANES] + value[:, LANES:]


def norms_kernel(
    gathered, spread, row_sums, linear, quadratic, edge_value, edge_field, early, late,
    packed, own_part, probe_part,
):
    even = lax.rem(lax.axis_index("lon"), 2) == 0
    corrections(gathered, spread, probe_part, even)
    wide = probe_part.shape[2]
    width = wide - LANES
    own_part[...] = probe_part[:, 24:72, :width]
    found = [late[6], late[7], early[0], late[8], late[9], early[1]] + [late[at] for at in range(6)]

    def wide_row(value):
        return jnp.broadcast_to(value, (8, width))

    def own(level, column, group):
        at = column * 24 + group * 8
        return probe_part[level, at : at + 8, :]

    for level in range(2):
        for column in range(2):
            pairs = {
                pair: wide_row(quadratic[level, column, at : at + 1, :]) for at, pair in enumerate(PAIRS)
            }
            for group in range(3):
                here = own(level, column + 1, group)
                terms = [
                    here[:, :width],
                    pltpu.roll(here, 1, 1)[:, :width],
                    pltpu.roll(here, wide - 1, 1)[:, :width],
                    own(1 - level, column + 1, group)[:, :width],
                ]
                at = column * 24 + group * 8
                cross = terms[0] * row_sums[level, at : at + 8, :]
                norm = jnp.zeros((8, width), F32)
                for one in range(4):
                    inside = terms[one] * pairs[one, one]
                    double = linear[level, column, group, one]
                    for two in range(one + 1, 4):
                        double = double + terms[two] * pairs[one, two]
                    norm = norm + terms[one] * (inside + 2.0 * double)
                for place in (2 * column, 2 * column + 1):
                    beyond = (0, 2, 1, 3)[place]
                    value = edge_value[place, level, group]
                    for kind, which in enumerate((level, 2, 3, 4)):
                        value = value + terms[kind] * wide_row(edge_field[place, which : which + 1, :])
                    value = value + own(level, beyond, group)[:, :width] * wide_row(
                        edge_field[place, 5:6, :]
                    )
                    norm = norm + (value * value)
                    mine = edge_value[place, level, group]
                    norm = norm - mine * mine
                found[6 + group] = found[6 + group] + cross[:, :LANES] + cross[:, LANES:]
                found[9 + group] = found[9 + group] + norm[:, :LANES] + norm[:, LANES:]
    lane = iota((8, LANES), 1)
    probe = iota((8, LANES), 0)
    out = jnp.zeros((8, LANES), F32)
    for kind in range(4):
        for group in range(3):
            total = jnp.broadcast_to(
                jnp.sum(found[kind * 3 + group], axis=1, keepdims=True), (8, LANES)
            )
            place = lane == (64 + kind if group == 2 else (kind * 2 + group) * 8 + probe)
            out = out + jnp.where(place, total, 0.0)
    packed[...] = jnp.broadcast_to(jnp.sum(out, axis=0, keepdims=True), packed.shape)


def finish_kernel(packed, early_part, later_part, basis, solution, diagonal, residual, ocean, bits, held, sems):
    _, lon_rows, width = solution.shape
    groups = lon_rows // 8
    total = jnp.broadcast_to(jnp.sum(packed[...], axis=0, keepdims=True), (8, LANES))
    lane = iota((8, LANES), 1)
    probe = iota((8, LANES), 0)

    def get(at):
        return jnp.concatenate([basis[at + group] for group in range(groups)], axis=0)

    def send(which, level):
        target = (solution, diagonal, residual)[which]
        copy = pltpu.make_async_copy(held.at[which, level], target.at[level], sems.at[which, level])
        copy.start()
        return copy

    def weights(group):
        found = []
        for kind in range(4):
            place = lane == (64 + kind if group == 2 else (kind * 2 + group) * 8 + probe)
            found.append(
                jnp.broadcast_to(
                    jnp.sum(jnp.where(place, total, 0.0), axis=1, keepdims=True), (8, LANES)
                )
            )
        gamma, norm, cross, second = found
        ratio = cross / norm
        rest = second - ratio * cross
        alive = rest > 0.0
        later = jnp.where(alive, (norm - ratio * gamma) / jnp.where(alive, rest, 1.0), 0.0)
        earlier = gamma / norm - later * ratio
        return (
            jnp.concatenate([earlier] * (width // LANES), axis=1),
            jnp.concatenate([later] * (width // LANES), axis=1),
        )

    wet = get(BASIS[4])
    keep(ocean, wet)
    for level in range(2):
        for word in range(2):
            bits[word, level] = get(BASIS[5] + (word * 2 + level) * groups).astype(jnp.int32)
    system = [weights(group) for group in range(3)]
    bit = jnp.left_shift(1, iota((8, width), 0))
    row = iota((lon_rows, width), 0)
    share = jnp.sum(system[0][0] + system[1][0], axis=0, keepdims=True)
    share = 2.0 * wet * jnp.broadcast_to(share, (lon_rows, width))
    earlier, later = system[2][0][0:1], system[2][1][0:1]
    copies = []
    for level in range(2):
        lines = [
            earlier * early_part[level, at : at + 1, :] + later * later_part[level, at : at + 1, :]
            for at in (16, 40)
        ]
        held[0, level] = (
            earlier * get(BASIS[1] + level * groups)
            + later * get(BASIS[2] + level * groups)
            + wet * jnp.where(row < BLK, lines[0], lines[1])
        )
        copies.append(send(0, level))
    for level in range(2):
        for column in range(2):
            coarse = []
            for word in range(2):
                at = column * 24 + word * 8
                coarse.append(
                    system[word][0] * early_part[level, at : at + 8, :]
                    + system[word][1] * later_part[level, at : at + 8, :]
                )

            def body(line, carry, coarse=coarse, level=level):
                signs, rest = None, None
                for word in range(2):
                    signed = jnp.where(
                        (row_of(bits.at[word, level], line) & bit) != 0, coarse[word], -coarse[word]
                    )
                    second = system[word][1] * basis[(level * 2 + word) * lon_rows + line]
                    signs = signed if signs is None else signs + signed
                    rest = second if rest is None else rest + second
                whole = same_row(ocean, line, 0) * signs + rest
                held[1, level, pl.ds(line, 1), :] = jnp.sum(whole, axis=0, keepdims=True)
                return carry

            lax.fori_loop(column * BLK, column * BLK + BLK, body, 0, unroll=BLK)
        bound = get(BASIS[3] + level * groups)
        spread = (held[1, level] + share * bound) / PROBES
        held[1, level] = spread
        copies.append(send(1, level))
        held[2, level] = held[0, level] / jnp.maximum(spread, bound)
        copies.append(send(2, level))
    for copy in copies:
        copy.wait()


def call(kernel, outs, scratch=(), outside=0):
    return functools.partial(_run, kernel, outs, scratch, outside)


def _run(kernel, outs, scratch, outside, *args):
    held = [pltpu.with_memory_space_constraint(array, pltpu.HBM) for array in args[:outside]]
    return pl.pallas_call(
        kernel,
        out_shape=outs,
        in_specs=[pl.BlockSpec(memory_space=pltpu.HBM)] * outside + vmem(len(args) - outside),
        out_specs=tuple(vmem(len(outs))),
        scratch_shapes=list(scratch),
        compiler_params=pltpu.CompilerParams(vmem_limit_bytes=24 << 20),
    )(*held, *args[outside:])


def per_device(observed, kappa_squared, probe_bits, land_sea, coarse_block_inverse):
    lon_rows, width = land_sea.shape
    wide = width + LANES
    tiles = wide // LANES
    rows = lon_rows + 2 * TOP
    lon_count = lax.axis_size("lon")
    lat_count = lax.axis_size("lat")
    evens = [(i, i + 1 - 2 * (i % 2)) for i in range(lon_count)]
    odds = [(i, (i - 1 + 2 * (i % 2)) % lon_count) for i in range(lon_count)]
    raw = (observed, kappa_squared, probe_bits, land_sea)
    inside = [pltpu.VMEM(array.shape, array.dtype) for array in raw]
    sems = pltpu.SemaphoreType.DMA((4,))

    to_odd, to_even, own, rhs_sums = call(
        prepare_kernel,
        (shape(48, width), shape(48, width), shape(96, LANES), shape(2, 48, width)),
        [*inside, pltpu.VMEM((width // LANES, lon_rows, LANES), F32), sems],
        4,
    )(*raw)
    from_odd = lax.ppermute(to_odd, "lon", odds)
    from_even = lax.ppermute(to_even, "lon", evens)
    natural = (tiles - 1, rows, LANES)
    spread, *base = call(
        base_kernel,
        (
            shape(2, LANES, wide),
            shape(*natural),
            shape(2, *natural),
            shape(2, *natural),
            shape(2, *natural),
            jax.ShapeDtypeStruct((2, 2, *natural), jnp.int32),
            shape(2, 2, lon_rows, 8, width),
        ),
        [
            *inside,
            pltpu.VMEM(coarse_block_inverse.shape, F32),
            pltpu.SemaphoreType.DMA((5,)),
        ],
        5,
    )(*raw, coarse_block_inverse)
    (merged,) = call(merge_kernel, (shape(96, LANES),))(own, from_odd, from_even)
    gathered = lax.all_gather(merged, "lat")
    probe_parts = pltpu.VMEM((2, 96, wide), F32)
    first_parts = pltpu.VMEM((2, tiles, rows, LANES), F32)
    image, first_image, to_odd, to_even, own_sums, row_sums, early, own_part, ocean, coef, jacobi = call(
        image_kernel,
        (
            shape(2, 2, lon_rows + 2, 8, wide),
            shape(2, 10, 8, wide),
            shape(24, LANES),
            shape(24, LANES),
            shape(48, LANES),
            shape(2, 48, width),
            shape(2, 8, LANES),
            shape(2, 48, width),
            shape(tiles, rows, LANES),
            shape(2, tiles, rows, LANES),
            shape(2, tiles, rows, LANES),
        ),
        [
            first_parts,
            pltpu.VMEM((2, 2, tiles, rows, LANES), jnp.int32),
            pltpu.VMEM((2, 2, lon_rows + 2 * HALO, 8, wide), F32),
            pltpu.VMEM((2, 2, lon_rows + 2 * HALO, 8, wide), F32),
            pltpu.VMEM((2, 14, 8, wide), F32),
            pltpu.VMEM((2, 14, 8, wide), F32),
            probe_parts,
            first_parts,
        ],
    )(*base, from_odd, from_even, gathered, spread)

    sums_odd = lax.ppermute(to_odd, "lon", odds)
    sums_even = lax.ppermute(to_even, "lon", evens)
    blocks = width // LANES
    linear, quadratic, edge_value, edge_field, late, basis = call(
        products_kernel,
        (
            shape(2, 2, 3, 4, 8, width),
            shape(2, 2, 16, width),
            shape(4, 2, 3, 8, width),
            shape(4, 8, width),
            shape(10, 8, LANES),
            shape(BASIS[-1], 8, width),
        ),
        [
            pltpu.VMEM((5, blocks, lon_rows, LANES), F32),
            pltpu.VMEM((2, 2, lon_rows, 8, width), F32),
            pltpu.VMEM((2, blocks, lon_rows, LANES), F32),
        ],
    )(image, first_image, ocean, coef, jacobi, base[3], base[4], own_part, rhs_sums, row_sums)
    sums = lax.all_gather(jnp.concatenate([sums_odd + own_sums[:24], sums_even + own_sums[24:]], axis=0), "lat")
    packed, later_part = call(
        norms_kernel, (shape(lon_count * lat_count, LANES), shape(2, 48, width)), [probe_parts]
    )(
        sums, spread, row_sums, linear, quadratic, edge_value, edge_field, early, late
    )
    everyone = lax.all_to_all(packed, ("lon", "lat"), 0, 0)
    return tuple(
        pl.pallas_call(
            finish_kernel,
            out_shape=(shape(2, lon_rows, width),) * 3,
            in_specs=vmem(4),
            out_specs=tuple([pl.BlockSpec(memory_space=pltpu.HBM)] * 3),
            scratch_shapes=[
                pltpu.VMEM((blocks, lon_rows, LANES), F32),
                pltpu.VMEM((2, 2, lon_rows, width), jnp.int32),
                pltpu.VMEM((3, 2, lon_rows, width), F32),
                pltpu.SemaphoreType.DMA((3, 2)),
            ],
            compiler_params=pltpu.CompilerParams(vmem_limit_bytes=24 << 20),
        )(everyone, own_part, later_part, basis)
    )


def solution(mesh):
    placed = (
        P(None, "lon", "lat"),
        P(None, "lon", "lat"),
        P(None, None, "lon", "lat"),
        P("lon", "lat"),
        P(),
    )
    return jax.shard_map(
        per_device,
        mesh=mesh,
        in_specs=placed,
        out_specs=(P(None, "lon", "lat"), P(None, "lon", "lat"), P(None, "lon", "lat")),
        check_vma=False,
    )
```
